256 devices in a mesh: node: 64 (over z, x, core), edge: 4 (over y).
Axes of the slice: x: 4, y: 4, z: 8, core: 2. Of those that a mesh axis runs over, the one named last changes fastest.
Arguments:
- teleport: float32 [131072, 128], P(('node', 'edge')), may hold values from -6 to 6
- cotangent: float32 [131072, 128], P(('node', 'edge')), may hold values from -6 to 6
- fetch_table: int32 [64, 128], replicated, may hold values from -1 to 7, as said below
- block_row: int32 [64, 192], P('node'), may hold values from 0 to 7
- block_slot: int32 [64, 192], P('node'), may hold values from 0 to 127, as said below
- values: bfloat16 [64, 192, 256, 256], P('node', None, 'edge'), may hold values from -0.078125 to 0.078125
Outputs:
- propagated: float32 [131072, 128], P(('node', 'edge'))
- teleport_grad: float32 [131072, 128], P(('node', 'edge'))
The draws below stay inside these ranges and needn't reach their ends.
Inputs may be any that keep to these rules, and one draw needn't show every extreme that they name: `fetch_table`: entry n, o * 2 + k names a node block index j of owner group o that group n reads in slot k, or is -1 for an empty slot. Within the 2 slots of one owner the live ones come first and name distinct blocks. One owner group has all 2 slots live in every row. `block_slot`: every entry names a live slot of the group's row of fetch_table, and every live slot of that row is named by at least one adjacency block of the group.
All inputs are finite; a program needn't handle non-finite values.
Results may differ from the reference program's by a relative error of at most 0.004.
Values may be sent and summed in bfloat16 or wider, within the bound.
A program may use at most 128 MiB of HBM per device.

```python
import jax
import jax.numpy as jnp
from jax import lax

HID = 128
BS = 256
CAP = 2
STEPS = 2
NB_DEV = 8
EB = 192
QUARTER = 64
NODES = 131072
N_NODE = 64
N_EDGE = 4


def fetch_plan(key):
    busiest = jax.random.randint(jax.random.fold_in(key, 11), (), 0, N_NODE)
    appeal = jax.random.randint(jax.random.fold_in(key, 12), (N_NODE,), 0, 4)
    jitter = jax.random.randint(jax.random.fold_in(key, 13), (N_NODE, N_NODE), 0, 3)
    live_count = jnp.clip(jitter + appeal[None, :] - 1, 0, CAP)
    owners = jnp.arange(N_NODE, dtype=jnp.int32)
    live_count = jnp.where(owners[None, :] == busiest, CAP, live_count)
    scores = jax.random.randint(jax.random.fold_in(key, 14), (N_NODE, N_NODE, NB_DEV), 0, 2 ** 20)
    scores = scores * NB_DEV + jnp.arange(NB_DEV, dtype=jnp.int32)[None, None, :]
    picked = jnp.argsort(scores, axis=-1)[:, :, :CAP].astype(jnp.int32)
    in_use = jnp.arange(CAP, dtype=jnp.int32)[None, None, :] < live_count[:, :, None]
    return jnp.where(in_use, picked, -1).reshape(N_NODE, N_NODE * CAP).astype(jnp.int32)


def draw_fetch_table(key, part):
    return fetch_plan(key)


def draw_block_slot(key, part):
    table = fetch_plan(key)
    slot_total = N_NODE * CAP
    live_mask = table >= 0
    slot_range = jnp.arange(slot_total, dtype=jnp.int32)[None, :]
    order_key = jnp.where(live_mask, 0, slot_total) + slot_range
    live_order = jnp.argsort(order_key, axis=1).astype(jnp.int32)
    live_total = jnp.sum(live_mask.astype(jnp.int32), axis=1)
    positions = jnp.arange(EB, dtype=jnp.int32)[None, :]
    spread = jax.random.randint(jax.random.fold_in(key, 21), (N_NODE, EB), 0, live_total[:, None])
    chosen_pos = jnp.where(positions < live_total[:, None], positions, spread)
    chosen = jnp.take_along_axis(live_order, chosen_pos, axis=1)
    mixing = jax.random.randint(jax.random.fold_in(key, 22), (N_NODE, EB), 0, 2 ** 20) * EB + positions
    shuffle = jnp.argsort(mixing, axis=1)
    return jnp.take_along_axis(chosen, shuffle, axis=1).astype(jnp.int32)


def with_ends(values, key, low, high):
    place = [jax.random.randint(jax.random.fold_in(key, axis), (), 0, length) for axis, length in enumerate(values.shape)]
    main_axis = values.shape.index(max(values.shape))
    next_to = place[:main_axis] + [(place[main_axis] + 1) % values.shape[main_axis]] + place[main_axis + 1:]
    return values.at[tuple(place)].set(low).at[tuple(next_to)].set(high)


def steps_of(own_key, extent, cuts, smallest, largest):
    def one(dim, blocks):
        heights = jax.random.uniform(jax.random.fold_in(jax.random.fold_in(own_key, 6), dim), (blocks,), jnp.float32, smallest / len(cuts), largest / len(cuts))
        return jnp.repeat(jnp.exp(heights), extent[dim] // blocks).reshape((-1,) + (1,) * (len(extent) - dim - 1))

    gain = one(*cuts[0])
    for cut in cuts[1:]:
        gain = gain * one(*cut)
    return gain


def gaussian(rng, dims, scale, bound, cuts=(), held_as=jnp.bfloat16):
    level = steps_of(rng, dims, cuts, -0.22, 0.18) if cuts else 1.0
    drawn = jax.random.normal(rng, dims, jnp.float32) * scale * level
    return jnp.minimum(jnp.maximum(drawn, -bound), bound).astype(held_as)


def setup_inputs(seed: int = 0) -> dict:
    key_of = jax.random.split(jax.random.key(seed), 7)
    return {
        "teleport": gaussian(key_of[0], (NODES, HID), 1.0, 6.0, ((0, 256),), jnp.float32),
        "cotangent": gaussian(key_of[1], (NODES, HID), 1.0, 6.0, ((0, 256),), jnp.float32),
        "fetch_table": draw_fetch_table(jax.random.fold_in(key_of[6], 71), 0),
        "block_row": with_ends(jax.random.randint(key_of[3], (N_NODE, EB), 0, NB_DEV), jax.random.fold_in(key_of[3], 1), 0, NB_DEV - 1).astype(jnp.int32),
        "block_slot": draw_block_slot(jax.random.fold_in(key_of[6], 71), 0),
        "values": gaussian(key_of[5], (N_NODE, EB, BS, BS), (BS * EB // NB_DEV) ** -0.5, 0.078125, ((0, 64), (2, 4))),
    }


def node_blocks(array):
    arranged = array.reshape(N_NODE, N_EDGE, NB_DEV, QUARTER, HID).transpose(0, 2, 1, 3, 4)
    return arranged.reshape(N_NODE * NB_DEV, BS, HID)


def node_order(blocks):
    arranged = blocks.reshape(N_NODE, NB_DEV, N_EDGE, QUARTER, HID).transpose(0, 2, 1, 3, 4)
    return arranged.reshape(NODES, HID)


def forward_apply(rounded, values, block_row, column_ids):
    def one_group(inputs):
        weights, row_ids, targets = inputs
        gathered = jnp.take(rounded, targets, axis=0).astype(jnp.float32)
        product = jnp.einsum("bcr,bch->brh", weights.astype(jnp.float32), gathered, precision=lax.Precision.HIGHEST)
        return jnp.zeros((NB_DEV, BS, HID), jnp.float32).at[row_ids].add(product)

    result = lax.map(one_group, (values, block_row, column_ids))
    return result.reshape(N_NODE * NB_DEV, BS, HID)


def transpose_apply(rounded, values, block_row, column_ids):
    def one_group(running, inputs):
        group_id, weights, row_ids, targets = inputs
        sources = jnp.take(rounded, group_id * NB_DEV + row_ids, axis=0).astype(jnp.float32)
        product = jnp.einsum("bcr,brh->bch", weights.astype(jnp.float32), sources, precision=lax.Precision.HIGHEST)
        return running.at[targets].add(product), None

    start_sum = jnp.zeros((N_NODE * NB_DEV, BS, HID), jnp.float32)
    group_ids = jnp.arange(N_NODE, dtype=jnp.int32)
    result, _ = lax.scan(one_group, start_sum, (group_ids, values, block_row, column_ids))
    return result


def reference(teleport, cotangent, fetch_table, block_row, block_slot, values):
    owner_part = (block_slot // CAP).astype(jnp.int32)
    local_part = jnp.take_along_axis(fetch_table, block_slot, axis=1).astype(jnp.int32)
    column_ids = (owner_part * NB_DEV + local_part).astype(jnp.int32)
    base = node_blocks(teleport)
    current = base
    for step_index in range(STEPS):
        rounded = current.astype(jnp.bfloat16)
        current = 0.9 * forward_apply(rounded, values, block_row, column_ids) + 0.1 * base
    adjoint = node_blocks(cotangent)
    gradient = 0.1 * adjoint
    for step_index in range(STEPS):
        rounded = adjoint.astype(jnp.bfloat16)
        adjoint = 0.9 * transpose_apply(rounded, values, block_row, column_ids)
        factor = 0.1 if step_index + 1 < STEPS else 1.0
        gradient = gradient + factor * adjoint
    return node_order(current), node_order(gradient)
```

```python
import functools

import jax
import jax.numpy as jnp
from jax import lax
from jax.experimental import pallas as pl
from jax.experimental.pallas import tpu as pltpu
from jax.sharding import Mesh
from jax.sharding import PartitionSpec as P

CAP = 2
STEPS = 2
Z_SIZE = 8
X_SIZE = 4
CORE_SIZE = 2
CHUNK = 16


def forward_kernel(rows_ref, slots_ref, v_ref, x_ref, out_ref):
    step = pl.program_id(0)

    @pl.when(step == 0)
    def _():
        out_ref[...] = jnp.zeros_like(out_ref)

    quarters, _, quarter, hidden = out_ref.shape

    def body(i, carry):
        b = step * CHUNK + i
        j = rows_ref[b]
        s = slots_ref[b]
        product = lax.dot_general(
            v_ref[i], x_ref[s], (((0,), (0,)), ((), ())), preferred_element_type=jnp.float32
        )
        out_ref[:, j] += product.reshape(quarters, quarter, hidden)
        return carry

    lax.fori_loop(0, CHUNK, body, 0)


def backward_kernel(rows_ref, slots_ref, v_ref, a_ref, out_ref):
    step = pl.program_id(0)

    @pl.when(step == 0)
    def _():
        out_ref[...] = jnp.zeros_like(out_ref)

    quarters, _, quarter, hidden = a_ref.shape

    def body(i, carry):
        b = step * CHUNK + i
        j = rows_ref[b]
        s = slots_ref[b]
        sources = a_ref[:, j].reshape(quarters * quarter, hidden)
        out_ref[s] += jnp.dot(v_ref[i], sources, preferred_element_type=jnp.float32)
        return carry

    lax.fori_loop(0, CHUNK, body, 0)


def forward_apply(rows, slots, weights, received, quarters):
    block_count, quarter, width = weights.shape
    hidden = received.shape[-1]
    blocks_dev = 8
    return pl.pallas_call(
        forward_kernel,
        out_shape=jax.ShapeDtypeStruct((quarters, blocks_dev, quarter, hidden), jnp.float32),
        grid_spec=pltpu.PrefetchScalarGridSpec(
            num_scalar_prefetch=2,
            grid=(block_count // CHUNK,),
            in_specs=[
                pl.BlockSpec((CHUNK, quarter, width), lambda i, r, s: (i, 0, 0)),
                pl.BlockSpec(received.shape, lambda i, r, s: (0, 0, 0)),
            ],
            out_specs=pl.BlockSpec(
                (quarters, blocks_dev, quarter, hidden), lambda i, r, s: (0, 0, 0, 0)
            ),
        ),
        compiler_params=pltpu.CompilerParams(dimension_semantics=("arbitrary",)),
    )(rows, slots, weights, received)


def backward_apply(rows, slots, weights, sources, slot_total):
    block_count, quarter, width = weights.shape
    hidden = sources.shape[-1]
    return pl.pallas_call(
        backward_kernel,
        out_shape=jax.ShapeDtypeStruct((slot_total, quarter, hidden), jnp.float32),
        grid_spec=pltpu.PrefetchScalarGridSpec(
            num_scalar_prefetch=2,
            grid=(block_count // CHUNK,),
            in_specs=[
                pl.BlockSpec((CHUNK, quarter, width), lambda i, r, s: (i, 0, 0)),
                pl.BlockSpec(sources.shape, lambda i, r, s: (0, 0, 0, 0)),
            ],
            out_specs=pl.BlockSpec((slot_total, quarter, hidden), lambda i, r, s: (0, 0, 0)),
        ),
        compiler_params=pltpu.CompilerParams(dimension_semantics=("arbitrary",)),
    )(rows, slots, weights, sources)


def per_device(teleport, cotangent, fetch_table, block_row, block_slot, values):
    row_count, hidden = teleport.shape
    quarter = values.shape[2]
    blocks_dev = row_count // quarter
    slot_total = fetch_table.shape[1]
    quarters = lax.axis_size("edge")
    row_peers = X_SIZE * CORE_SIZE
    z_me = lax.axis_index("z")
    x_me = lax.axis_index("x")
    c_me = lax.axis_index("c")
    weights = values[0]
    row_ids = block_row[0]
    slot_ids = block_slot[0]

    owner = slot_ids // CAP
    placed_slots = (
        ((owner // CORE_SIZE % X_SIZE * CORE_SIZE + owner % CORE_SIZE) * Z_SIZE + owner // (CORE_SIZE * X_SIZE))
        * CAP
        + slot_ids % CAP
    ).astype(jnp.int32)

    peer_range = jnp.arange(row_peers, dtype=jnp.int32)
    z_range = jnp.arange(Z_SIZE, dtype=jnp.int32)
    peer_groups = (z_me * X_SIZE + peer_range // CORE_SIZE) * CORE_SIZE + peer_range % CORE_SIZE
    line_owners = (z_range * X_SIZE + x_me) * CORE_SIZE + c_me
    table_cols = line_owners[:, None] * CAP + jnp.arange(CAP, dtype=jnp.int32)[None, :]
    wanted = fetch_table[peer_groups[:, None, None], table_cols[None, :, :]]
    send_index = (z_range[None, :, None] * blocks_dev + jnp.maximum(wanted, 0)).reshape(-1)
    wanted_hot = (
        wanted.transpose(1, 0, 2).reshape(Z_SIZE, 1, row_peers * CAP)
        == jnp.arange(blocks_dev, dtype=jnp.int32)[None, :, None]
    ).astype(jnp.float32)

    current = teleport
    for step_index in range(STEPS):
        rounded = current.astype(jnp.bfloat16).reshape(blocks_dev, quarter, hidden)
        line_blocks = lax.all_gather(rounded, "z", axis=0, tiled=True)
        outgoing = jnp.take(line_blocks, send_index, axis=0)
        received = lax.all_to_all(
            outgoing, ("x", "c"), split_axis=0, concat_axis=0, tiled=True
        )
        partial = forward_apply(row_ids, placed_slots, weights, received, quarters)
        summed = lax.psum_scatter(
            partial.reshape(quarters * row_count, hidden), "edge", scatter_dimension=0, tiled=True
        )
        current = 0.9 * summed + 0.1 * teleport

    adjoint = cotangent
    gradient = 0.1 * cotangent
    for step_index in range(STEPS):
        rounded = adjoint.astype(jnp.bfloat16).reshape(1, blocks_dev, quarter, hidden)
        whole_rows = lax.all_gather(rounded, "edge", axis=0, tiled=True)
        slot_sums = backward_apply(row_ids, placed_slots, weights, whole_rows, slot_total)
        arrived = lax.all_to_all(
            slot_sums, ("x", "c"), split_axis=0, concat_axis=0, tiled=True
        )
        arrived = arrived.reshape(row_peers, Z_SIZE, CAP, quarter * hidden)
        arrived = arrived.transpose(1, 0, 2, 3).reshape(Z_SIZE, row_peers * CAP, quarter * hidden)
        dense = jnp.einsum(
            "zjq,zqd->zjd", wanted_hot, arrived, precision=lax.Precision.HIGHEST
        )
        owned = lax.psum_scatter(dense, "z", scatter_dimension=0, tiled=True)
        adjoint = 0.9 * owned.reshape(row_count, hidden)
        factor = 0.1 if step_index + 1 < STEPS else 1.0
        gradient = gradient + factor * adjoint
    return (current, gradient)


def solution(mesh):
    devices = mesh.devices.reshape(Z_SIZE, X_SIZE, CORE_SIZE, mesh.shape["edge"])
    fine = Mesh(devices, ("z", "x", "c", "edge"))
    node = ("z", "x", "c")
    placed = (
        P((*node, "edge"), None),
        P((*node, "edge"), None),
        P(),
        P(node, None),
        P(node, None),
        P(node, None, "edge", None),
    )
    return jax.shard_map(
        per_device,
        mesh=fine,
        in_specs=placed,
        out_specs=(P((*node, "edge"), None), P((*node, "edge"), None)),
        check_vma=False,
    )
```

```python
import jax
import jax.numpy as jnp
from jax import lax
from jax.experimental import pallas as pl
from jax.experimental.pallas import tpu as pltpu
from jax.sharding import Mesh
from jax.sharding import PartitionSpec as P

CAP = 2
STEPS = 2
Z_SIZE = 8
X_SIZE = 4
CORE_SIZE = 2
GROUP = 4
GROUPS_PER_STEP = 8


def forward_kernel(rows_ref, slots_ref, vt_ref, x_ref, out_ref):
    step = pl.program_id(0)

    @pl.when(step == 0)
    def _():
        out_ref[...] = jnp.zeros_like(out_ref)

    quarters, _, quarter, hidden = out_ref.shape

    def body(i, carry):
        g = step * GROUPS_PER_STEP + i
        j = rows_ref[g]
        sources = jnp.concatenate(
            [x_ref[slots_ref[g * GROUP + m]] for m in range(GROUP)], axis=0
        )
        product = jnp.dot(vt_ref[i], sources, preferred_element_type=jnp.float32)
        out_ref[:, j] += product.reshape(quarters, quarter, hidden)
        return carry

    lax.fori_loop(0, GROUPS_PER_STEP, body, 0)


def backward_kernel(rows_ref, slots_ref, v_ref, a_ref, out_ref):
    step = pl.program_id(0)

    @pl.when(step == 0)
    def _():
        out_ref[...] = jnp.zeros_like(out_ref)

    quarters, _, quarter, hidden = a_ref.shape

    def body(i, carry):
        g = step * GROUPS_PER_STEP + i
        j = rows_ref[g]
        sources = a_ref[:, j].reshape(quarters * quarter, hidden)
        product = jnp.dot(v_ref[i], sources, preferred_element_type=jnp.float32)
        for m in range(GROUP):
            s = slots_ref[g * GROUP + m]
            out_ref[s] += product[m * quarter:(m + 1) * quarter]
        return carry

    lax.fori_loop(0, GROUPS_PER_STEP, body, 0)


def combine_kernel(want_ref, arrived_ref, out_ref):
    out_ref[...] = jnp.zeros_like(out_ref)
    lines = out_ref.shape[0]

    def body(q, carry):
        j = want_ref[q]

        @pl.when(j >= 0)
        def _():
            out_ref[q // CAP % lines, j] += arrived_ref[q]

        return carry

    lax.fori_loop(0, arrived_ref.shape[0], body, 0)


def forward_apply(rows, slots, weights_t, received, quarters, blocks_dev):
    group_count, width, depth = weights_t.shape
    quarter, hidden = received.shape[1:]
    return pl.pallas_call(
        forward_kernel,
        out_shape=jax.ShapeDtypeStruct((quarters, blocks_dev, quarter, hidden), jnp.float32),
        grid_spec=pltpu.PrefetchScalarGridSpec(
            num_scalar_prefetch=2,
            grid=(group_count // GROUPS_PER_STEP,),
            in_specs=[
                pl.BlockSpec((GROUPS_PER_STEP, width, depth), lambda i, r, s: (i, 0, 0)),
                pl.BlockSpec(received.shape, lambda i, r, s: (0, 0, 0)),
            ],
            out_specs=pl.BlockSpec(
                (quarters, blocks_dev, quarter, hidden), lambda i, r, s: (0, 0, 0, 0)
            ),
        ),
        compiler_params=pltpu.CompilerParams(dimension_semantics=("arbitrary",)),
    )(rows, slots, weights_t, received)


def backward_apply(rows, slots, weights_g, sources, slot_total):
    group_count, depth, width = weights_g.shape
    quarter, hidden = sources.shape[2:]
    return pl.pallas_call(
        backward_kernel,
        out_shape=jax.ShapeDtypeStruct((slot_total, quarter, hidden), jnp.float32),
        grid_spec=pltpu.PrefetchScalarGridSpec(
            num_scalar_prefetch=2,
            grid=(group_count // GROUPS_PER_STEP,),
            in_specs=[
                pl.BlockSpec((GROUPS_PER_STEP, depth, width), lambda i, r, s: (i, 0, 0)),
                pl.BlockSpec(sources.shape, lambda i, r, s: (0, 0, 0, 0)),
            ],
            out_specs=pl.BlockSpec((slot_total, quarter, hidden), lambda i, r, s: (0, 0, 0)),
        ),
        compiler_params=pltpu.CompilerParams(dimension_semantics=("arbitrary",)),
    )(rows, slots, weights_g, sources)


def combine_apply(wanted, arrived, blocks_dev):
    slot_total, quarter, hidden = arrived.shape
    lines = slot_total // (CAP * X_SIZE * CORE_SIZE)
    return pl.pallas_call(
        combine_kernel,
        out_shape=jax.ShapeDtypeStruct((lines, blocks_dev, quarter, hidden), jnp.float32),
        grid_spec=pltpu.PrefetchScalarGridSpec(
            num_scalar_prefetch=1,
            grid=(1,),
            in_specs=[pl.BlockSpec(arrived.shape, lambda i, w: (0, 0, 0))],
            out_specs=pl.BlockSpec(
                (lines, blocks_dev, quarter, hidden), lambda i, w: (0, 0, 0, 0)
            ),
        ),
    )(wanted, arrived)


def grouping(row_ids, blocks_dev):
    block_count = row_ids.shape[0]
    group_count = block_count // GROUP + blocks_dev
    order = jnp.argsort(row_ids, stable=True).astype(jnp.int32)
    sorted_rows = row_ids[order]
    counts = jnp.sum(
        (row_ids[None, :] == jnp.arange(blocks_dev, dtype=jnp.int32)[:, None]).astype(jnp.int32), axis=1
    )
    groups_per_row = (counts + GROUP - 1) // GROUP
    group_end = jnp.cumsum(groups_per_row)
    group_start = group_end - groups_per_row
    row_start = jnp.cumsum(counts) - counts
    rank = jnp.arange(block_count, dtype=jnp.int32) - row_start[sorted_rows]
    position = group_start[sorted_rows] * GROUP + rank
    member = jnp.full((group_count * GROUP,), block_count, jnp.int32).at[position].set(order)
    group_range = jnp.arange(group_count, dtype=jnp.int32)
    group_row = jnp.minimum(
        jnp.sum((group_range[:, None] >= group_end[None, :]).astype(jnp.int32), axis=1), blocks_dev - 1
    ).astype(jnp.int32)
    return member, group_row


def per_device(teleport, cotangent, fetch_table, block_row, block_slot, values):
    row_count, hidden = teleport.shape
    quarter = values.shape[2]
    blocks_dev = row_count // quarter
    slot_total = fetch_table.shape[1]
    quarters = lax.axis_size("edge")
    row_peers = X_SIZE * CORE_SIZE
    z_me = lax.axis_index("z")
    x_me = lax.axis_index("x")
    c_me = lax.axis_index("c")
    weights = values[0]
    row_ids = block_row[0]
    slot_ids = block_slot[0]

    owner = slot_ids // CAP
    placed_slots = (
        ((owner // CORE_SIZE % X_SIZE * CORE_SIZE + owner % CORE_SIZE) * Z_SIZE + owner // (CORE_SIZE * X_SIZE))
        * CAP
        + slot_ids % CAP
    ).astype(jnp.int32)

    peer_range = jnp.arange(row_peers, dtype=jnp.int32)
    z_range = jnp.arange(Z_SIZE, dtype=jnp.int32)
    peer_groups = (z_me * X_SIZE + peer_range // CORE_SIZE) * CORE_SIZE + peer_range % CORE_SIZE
    line_owners = (z_range * X_SIZE + x_me) * CORE_SIZE + c_me
    table_cols = line_owners[:, None] * CAP + jnp.arange(CAP, dtype=jnp.int32)[None, :]
    wanted = fetch_table[peer_groups[:, None, None], table_cols[None, :, :]]
    send_index = (z_range[None, :, None] * blocks_dev + jnp.maximum(wanted, 0)).reshape(-1)

    member, group_row = grouping(row_ids, blocks_dev)
    member_slot = jnp.concatenate([placed_slots, jnp.zeros((1,), jnp.int32)])[member]
    padded = jnp.concatenate([weights, jnp.zeros((1,) + weights.shape[1:], weights.dtype)])[member]
    group_count = member.shape[0] // GROUP
    width = weights.shape[2]
    weights_g = padded.reshape(group_count, GROUP * quarter, width)
    weights_t = (
        padded.reshape(group_count, GROUP, quarter, width)
        .transpose(0, 3, 1, 2)
        .reshape(group_count, width, GROUP * quarter)
    )
    wanted_flat = wanted.reshape(-1)

    current = teleport
    for step_index in range(STEPS):
        rounded = current.astype(jnp.bfloat16).reshape(blocks_dev, quarter, hidden)
        line_blocks = lax.all_gather(rounded, "z", axis=0, tiled=True)
        outgoing = jnp.take(line_blocks, send_index, axis=0)
        received = lax.all_to_all(
            outgoing, ("x", "c"), split_axis=0, concat_axis=0, tiled=True
        )
        partial = forward_apply(group_row, member_slot, weights_t, received, quarters, blocks_dev)
        summed = lax.psum_scatter(
            partial.reshape(quarters * row_count, hidden), "edge", scatter_dimension=0, tiled=True
        )
        current = 0.9 * summed + 0.1 * teleport

    adjoint = cotangent
    gradient = 0.1 * cotangent
    for step_index in range(STEPS):
        rounded = adjoint.astype(jnp.bfloat16).reshape(1, blocks_dev, quarter, hidden)
        whole_rows = lax.all_gather(rounded, "edge", axis=0, tiled=True)
        slot_sums = backward_apply(group_row, member_slot, weights_g, whole_rows, slot_total)
        arrived = lax.all_to_all(
            slot_sums, ("x", "c"), split_axis=0, concat_axis=0, tiled=True
        )
        dense = combine_apply(wanted_flat, arrived, blocks_dev)
        owned = lax.psum_scatter(dense, "z", scatter_dimension=0, tiled=True)
        adjoint = 0.9 * owned.reshape(row_count, hidden)
        factor = 0.1 if step_index + 1 < STEPS else 1.0
        gradient = gradient + factor * adjoint
    return (current, gradient)


def solution(mesh):
    devices = mesh.devices.reshape(Z_SIZE, X_SIZE, CORE_SIZE, mesh.shape["edge"])
    fine = Mesh(devices, ("z", "x", "c", "edge"))
    node = ("z", "x", "c")
    placed = (
        P((*node, "edge"), None),
        P((*node, "edge"), None),
        P(),
        P(node, None),
        P(node, None),
        P(node, None, "edge", None),
    )
    return jax.shard_map(
        per_device,
        mesh=fine,
        in_specs=placed,
        out_specs=(P((*node, "edge"), None), P((*node, "edge"), None)),
        check_vma=False,
    )
```

```python
import functools

import jax
import jax.numpy as jnp
from jax import lax
from jax.experimental import pallas as pl
from jax.experimental.pallas import tpu as pltpu
from jax.sharding import Mesh
from jax.sharding import PartitionSpec as P

MESH = pl.DeviceIdType.MESH

CAP = 2
STEPS = 2
Z_SIZE = 8
X_SIZE = 4
CORE_SIZE = 2
GROUP = 4
GROUPS_PER_STEP = 8


def forward_kernel(rows_ref, slots_ref, vt_ref, x_ref, out_ref):
    step = pl.program_id(0)

    @pl.when(step == 0)
    def _():
        out_ref[...] = jnp.zeros_like(out_ref)

    quarters, _, quarter, hidden = out_ref.shape

    def body(i, carry):
        g = step * GROUPS_PER_STEP + i
        j = rows_ref[g]
        sources = jnp.concatenate(
            [x_ref[slots_ref[g * GROUP + m]] for m in range(GROUP)], axis=0
        )
        product = jnp.dot(vt_ref[i], sources, preferred_element_type=jnp.float32)
        out_ref[:, j] += product.reshape(quarters, quarter, hidden)
        return carry

    lax.fori_loop(0, GROUPS_PER_STEP, body, 0)


def backward_kernel(rows_ref, slots_ref, v_ref, a_ref, out_ref):
    step = pl.program_id(0)

    @pl.when(step == 0)
    def _():
        out_ref[...] = jnp.zeros_like(out_ref)

    quarters, _, quarter, hidden = a_ref.shape

    def body(i, carry):
        g = step * GROUPS_PER_STEP + i
        j = rows_ref[g]
        sources = a_ref[:, j].reshape(quarters * quarter, hidden)
        product = jnp.dot(v_ref[i], sources, preferred_element_type=jnp.float32)
        for m in range(GROUP):
            s = slots_ref[g * GROUP + m]
            out_ref[s] += product[m * quarter:(m + 1) * quarter]
        return carry

    lax.fori_loop(0, GROUPS_PER_STEP, body, 0)


def combine_kernel(want_ref, arrived_ref, out_ref):
    out_ref[...] = jnp.zeros_like(out_ref)
    lines = out_ref.shape[0]

    def body(q, carry):
        j = want_ref[q]

        @pl.when(j >= 0)
        def _():
            out_ref[q // CAP % lines, j] += arrived_ref[q]

        return carry

    lax.fori_loop(0, arrived_ref.shape[0], body, 0)


def edge_exchange_kernel(reduce, x_ref, out_ref, held, send_sem, recv_sem):
    count = held.shape[0]
    me = lax.axis_index("edge")
    barrier = pltpu.get_barrier_semaphore()
    for d in range(1, count):
        pl.semaphore_signal(
            barrier, inc=1, device_id={"edge": lax.rem(me + d, count)}, device_id_type=MESH
        )
    pl.semaphore_wait(barrier, count - 1)
    copies = []
    for d in range(1, count):
        peer = lax.rem(me + d, count)
        copy = pltpu.make_async_remote_copy(
            src_ref=x_ref.at[peer] if reduce else x_ref.at[0],
            dst_ref=held.at[me],
            send_sem=send_sem.at[d],
            recv_sem=recv_sem.at[d],
            device_id={"edge": peer},
            device_id_type=MESH,
        )
        copy.start()
        copies.append(copy)
    held[me] = x_ref[me] if reduce else x_ref[0]
    for copy in copies:
        copy.wait()
    if reduce:
        total = held[0]
        for q in range(1, count):
            total = total + held[q]
        out_ref[...] = total
    else:
        out_ref[...] = held[...]


def edge_exchange(chunks, count, reduce, collective_id):
    piece = chunks.shape[1:]
    out_shape = piece if reduce else (count,) + piece
    return pl.pallas_call(
        functools.partial(edge_exchange_kernel, reduce),
        out_shape=jax.ShapeDtypeStruct(out_shape, chunks.dtype),
        in_specs=[pl.BlockSpec(memory_space=pltpu.VMEM)],
        out_specs=pl.BlockSpec(memory_space=pltpu.VMEM),
        scratch_shapes=[
            pltpu.VMEM((count,) + piece, chunks.dtype),
            pltpu.SemaphoreType.DMA((count,)),
            pltpu.SemaphoreType.DMA((count,)),
        ],
        compiler_params=pltpu.CompilerParams(collective_id=collective_id, has_side_effects=True),
    )(chunks)


def forward_apply(rows, slots, weights_t, received, quarters, blocks_dev):
    group_count, width, depth = weights_t.shape
    quarter, hidden = received.shape[1:]
    return pl.pallas_call(
        forward_kernel,
        out_shape=jax.ShapeDtypeStruct((quarters, blocks_dev, quarter, hidden), jnp.float32),
        grid_spec=pltpu.PrefetchScalarGridSpec(
            num_scalar_prefetch=2,
            grid=(group_count // GROUPS_PER_STEP,),
            in_specs=[
                pl.BlockSpec((GROUPS_PER_STEP, width, depth), lambda i, r, s: (i, 0, 0)),
                pl.BlockSpec(received.shape, lambda i, r, s: (0, 0, 0)),
            ],
            out_specs=pl.BlockSpec(
                (quarters, blocks_dev, quarter, hidden), lambda i, r, s: (0, 0, 0, 0)
            ),
        ),
        compiler_params=pltpu.CompilerParams(dimension_semantics=("arbitrary",)),
    )(rows, slots, weights_t, received)


def backward_apply(rows, slots, weights_g, sources, slot_total):
    group_count, depth, width = weights_g.shape
    quarter, hidden = sources.shape[2:]
    return pl.pallas_call(
        backward_kernel,
        out_shape=jax.ShapeDtypeStruct((slot_total, quarter, hidden), jnp.float32),
        grid_spec=pltpu.PrefetchScalarGridSpec(
            num_scalar_prefetch=2,
            grid=(group_count // GROUPS_PER_STEP,),
            in_specs=[
                pl.BlockSpec((GROUPS_PER_STEP, depth, width), lambda i, r, s: (i, 0, 0)),
                pl.BlockSpec(sources.shape, lambda i, r, s: (0, 0, 0, 0)),
            ],
            out_specs=pl.BlockSpec((slot_total, quarter, hidden), lambda i, r, s: (0, 0, 0)),
        ),
        compiler_params=pltpu.CompilerParams(dimension_semantics=("arbitrary",)),
    )(rows, slots, weights_g, sources)


def combine_apply(wanted, arrived, blocks_dev):
    slot_total, quarter, hidden = arrived.shape
    lines = slot_total // (CAP * X_SIZE * CORE_SIZE)
    return pl.pallas_call(
        combine_kernel,
        out_shape=jax.ShapeDtypeStruct((lines, blocks_dev, quarter, hidden), jnp.float32),
        grid_spec=pltpu.PrefetchScalarGridSpec(
            num_scalar_prefetch=1,
            grid=(1,),
            in_specs=[pl.BlockSpec(arrived.shape, lambda i, w: (0, 0, 0))],
            out_specs=pl.BlockSpec(
                (lines, blocks_dev, quarter, hidden), lambda i, w: (0, 0, 0, 0)
            ),
        ),
    )(wanted, arrived)


def grouping(row_ids, blocks_dev):
    block_count = row_ids.shape[0]
    group_count = block_count // GROUP + blocks_dev
    order = jnp.argsort(row_ids, stable=True).astype(jnp.int32)
    sorted_rows = row_ids[order]
    counts = jnp.sum(
        (row_ids[None, :] == jnp.arange(blocks_dev, dtype=jnp.int32)[:, None]).astype(jnp.int32), axis=1
    )
    groups_per_row = (counts + GROUP - 1) // GROUP
    group_end = jnp.cumsum(groups_per_row)
    group_start = group_end - groups_per_row
    row_start = jnp.cumsum(counts) - counts
    rank = jnp.arange(block_count, dtype=jnp.int32) - row_start[sorted_rows]
    position = group_start[sorted_rows] * GROUP + rank
    member = jnp.full((group_count * GROUP,), block_count, jnp.int32).at[position].set(order)
    group_range = jnp.arange(group_count, dtype=jnp.int32)
    group_row = jnp.minimum(
        jnp.sum((group_range[:, None] >= group_end[None, :]).astype(jnp.int32), axis=1), blocks_dev - 1
    ).astype(jnp.int32)
    return member, group_row


def per_device(teleport, cotangent, fetch_table, block_row, block_slot, values):
    row_count, hidden = teleport.shape
    quarter = values.shape[2]
    blocks_dev = row_count // quarter
    slot_total = fetch_table.shape[1]
    quarters = lax.axis_size("edge")
    row_peers = X_SIZE * CORE_SIZE
    z_me = lax.axis_index("z")
    x_me = lax.axis_index("x")
    c_me = lax.axis_index("c")
    weights = values[0]
    row_ids = block_row[0]
    slot_ids = block_slot[0]

    owner = slot_ids // CAP
    placed_slots = (
        ((owner // CORE_SIZE % X_SIZE * CORE_SIZE + owner % CORE_SIZE) * Z_SIZE + owner // (CORE_SIZE * X_SIZE))
        * CAP
        + slot_ids % CAP
    ).astype(jnp.int32)

    peer_range = jnp.arange(row_peers, dtype=jnp.int32)
    z_range = jnp.arange(Z_SIZE, dtype=jnp.int32)
    peer_groups = (z_me * X_SIZE + peer_range // CORE_SIZE) * CORE_SIZE + peer_range % CORE_SIZE
    line_owners = (z_range * X_SIZE + x_me) * CORE_SIZE + c_me
    table_cols = line_owners[:, None] * CAP + jnp.arange(CAP, dtype=jnp.int32)[None, :]
    wanted = fetch_table[peer_groups[:, None, None], table_cols[None, :, :]]
    send_index = (z_range[None, :, None] * blocks_dev + jnp.maximum(wanted, 0)).reshape(-1)

    member, group_row = grouping(row_ids, blocks_dev)
    member_slot = jnp.concatenate([placed_slots, jnp.zeros((1,), jnp.int32)])[member]
    padded = jnp.take(weights, member, axis=0, mode="fill", fill_value=0)
    group_count = member.shape[0] // GROUP
    width = weights.shape[2]
    weights_g = padded.reshape(group_count, GROUP * quarter, width)
    weights_t = (
        padded.reshape(group_count, GROUP, quarter, width)
        .transpose(0, 3, 1, 2)
        .reshape(group_count, width, GROUP * quarter)
    )
    wanted_flat = wanted.reshape(-1)

    current = teleport
    for step_index in range(STEPS):
        rounded = current.astype(jnp.bfloat16).reshape(blocks_dev, quarter, hidden)
        line_blocks = lax.all_gather(rounded, "z", axis=0, tiled=True)
        outgoing = jnp.take(line_blocks, send_index, axis=0)
        received = lax.all_to_all(
            outgoing, ("x", "c"), split_axis=0, concat_axis=0, tiled=True
        )
        partial = forward_apply(group_row, member_slot, weights_t, received, quarters, blocks_dev)
        summed = edge_exchange(partial, quarters, True, 1)
        current = 0.9 * summed.reshape(row_count, hidden) + 0.1 * teleport

    adjoint = cotangent
    gradient = 0.1 * cotangent
    for step_index in range(STEPS):
        rounded = adjoint.astype(jnp.bfloat16).reshape(1, blocks_dev, quarter, hidden)
        whole_rows = edge_exchange(rounded, quarters, False, 2)
        slot_sums = backward_apply(group_row, member_slot, weights_g, whole_rows, slot_total)
        arrived = lax.all_to_all(
            slot_sums, ("x", "c"), split_axis=0, concat_axis=0, tiled=True
        )
        dense = combine_apply(wanted_flat, arrived, blocks_dev)
        owned = lax.psum_scatter(dense, "z", scatter_dimension=0, tiled=True)
        adjoint = 0.9 * owned.reshape(row_count, hidden)
        factor = 0.1 if step_index + 1 < STEPS else 1.0
        gradient = gradient + factor * adjoint
    return (current, gradient)


def solution(mesh):
    devices = mesh.devices.reshape(Z_SIZE, X_SIZE, CORE_SIZE, mesh.shape["edge"])
    fine = Mesh(devices, ("z", "x", "c", "edge"))
    node = ("z", "x", "c")
    placed = (
        P((*node, "edge"), None),
        P((*node, "edge"), None),
        P(),
        P(node, None),
        P(node, None),
        P(node, None, "edge", None),
    )
    return jax.shard_map(
        per_device,
        mesh=fine,
        in_specs=placed,
        out_specs=(P((*node, "edge"), None), P((*node, "edge"), None)),
        check_vma=False,
    )
```

```python
import functools

import jax
import jax.numpy as jnp
from jax import lax
from jax.experimental import pallas as pl
from jax.experimental.pallas import tpu as pltpu
from jax.sharding import Mesh
from jax.sharding import PartitionSpec as P

MESH = pl.DeviceIdType.MESH

CAP = 2
STEPS = 2
Z_SIZE = 8
X_SIZE = 4
CORE_SIZE = 2
GROUP = 4


def fetch_group(members_ref, v_hbm, vbuf, sems, g, slot):
    last = v_hbm.shape[0] - 1
    for m in range(GROUP):
        b = jnp.minimum(members_ref[g * GROUP + m], last)
        pltpu.make_async_copy(v_hbm.at[b], vbuf.at[slot, m], sems.at[slot, m]).start()


def wait_group(v_hbm, vbuf, sems, slot):
    for m in range(GROUP):
        pltpu.make_async_copy(v_hbm.at[0], vbuf.at[slot, m], sems.at[slot, m]).wait()


def forward_kernel(rows_ref, members_ref, slots_ref, v_hbm, x_ref, out_ref, vbuf, sems):
    group_count = rows_ref.shape[0]
    block_count = v_hbm.shape[0]
    quarters, _, quarter, hidden = out_ref.shape
    out_ref[...] = jnp.zeros_like(out_ref)
    fetch_group(members_ref, v_hbm, vbuf, sems, 0, 0)

    def body(g, carry):
        slot = g % 2
        wait_group(v_hbm, vbuf, sems, slot)

        @pl.when(g + 1 < group_count)
        def _():
            fetch_group(members_ref, v_hbm, vbuf, sems, g + 1, 1 - slot)

        j = rows_ref[g]
        pieces = []
        for m in range(GROUP):
            valid = members_ref[g * GROUP + m] < block_count
            piece = x_ref[slots_ref[g * GROUP + m]]
            pieces.append(jnp.where(valid, piece, jnp.zeros_like(piece)))
        sources = jnp.concatenate(pieces, axis=0)
        weights = vbuf[slot].reshape(GROUP * quarter, vbuf.shape[-1])
        product = lax.dot_general(
            weights, sources, (((0,), (0,)), ((), ())), preferred_element_type=jnp.float32
        )
        out_ref[:, j] += product.reshape(quarters, quarter, hidden)
        return carry

    lax.fori_loop(0, group_count, body, 0)


def backward_kernel(rows_ref, members_ref, slots_ref, v_hbm, a_ref, out_ref, vbuf, sems):
    group_count = rows_ref.shape[0]
    block_count = v_hbm.shape[0]
    quarters, _, quarter, hidden = a_ref.shape
    out_ref[...] = jnp.zeros_like(out_ref)
    fetch_group(members_ref, v_hbm, vbuf, sems, 0, 0)

    def body(g, carry):
        slot = g % 2
        wait_group(v_hbm, vbuf, sems, slot)

        @pl.when(g + 1 < group_count)
        def _():
            fetch_group(members_ref, v_hbm, vbuf, sems, g + 1, 1 - slot)

        j = rows_ref[g]
        sources = a_ref[:, j].reshape(quarters * quarter, hidden)
        weights = vbuf[slot].reshape(GROUP * quarter, vbuf.shape[-1])
        product = jnp.dot(weights, sources, preferred_element_type=jnp.float32)
        for m in range(GROUP):
            s = slots_ref[g * GROUP + m]

            @pl.when(members_ref[g * GROUP + m] < block_count)
            def _():
                out_ref[s] += product[m * quarter:(m + 1) * quarter]

        return carry

    lax.fori_loop(0, group_count, body, 0)


def combine_kernel(want_ref, arrived_ref, out_ref):
    out_ref[...] = jnp.zeros_like(out_ref)
    lines = out_ref.shape[0]

    def body(q, carry):
        j = want_ref[q]

        @pl.when(j >= 0)
        def _():
            out_ref[q // CAP % lines, j] += arrived_ref[q]

        return carry

    lax.fori_loop(0, arrived_ref.shape[0], body, 0)


def edge_exchange_kernel(reduce, x_ref, out_ref, held, send_sem, recv_sem):
    count = held.shape[0]
    me = lax.axis_index("edge")
    barrier = pltpu.get_barrier_semaphore()
    for d in range(1, count):
        pl.semaphore_signal(
            barrier, inc=1, device_id={"edge": lax.rem(me + d, count)}, device_id_type=MESH
        )
    pl.semaphore_wait(barrier, count - 1)
    copies = []
    for d in range(1, count):
        peer = lax.rem(me + d, count)
        copy = pltpu.make_async_remote_copy(
            src_ref=x_ref.at[peer] if reduce else x_ref.at[0],
            dst_ref=held.at[me],
            send_sem=send_sem.at[d],
            recv_sem=recv_sem.at[d],
            device_id={"edge": peer},
            device_id_type=MESH,
        )
        copy.start()
        copies.append(copy)
    held[me] = x_ref[me] if reduce else x_ref[0]
    for copy in copies:
        copy.wait()
    if reduce:
        total = held[0]
        for q in range(1, count):
            total = total + held[q]
        out_ref[...] = total
    else:
        out_ref[...] = held[...]


def edge_exchange(chunks, count, reduce, collective_id):
    piece = chunks.shape[1:]
    out_shape = piece if reduce else (count,) + piece
    return pl.pallas_call(
        functools.partial(edge_exchange_kernel, reduce),
        out_shape=jax.ShapeDtypeStruct(out_shape, chunks.dtype),
        in_specs=[pl.BlockSpec(memory_space=pltpu.VMEM)],
        out_specs=pl.BlockSpec(memory_space=pltpu.VMEM),
        scratch_shapes=[
            pltpu.VMEM((count,) + piece, chunks.dtype),
            pltpu.SemaphoreType.DMA((count,)),
            pltpu.SemaphoreType.DMA((count,)),
        ],
        compiler_params=pltpu.CompilerParams(collective_id=collective_id, has_side_effects=True),
    )(chunks)


def block_apply(kernel, rows, members, slots, weights, dense, out_shape):
    block_count, quarter, width = weights.shape
    return pl.pallas_call(
        kernel,
        out_shape=jax.ShapeDtypeStruct(out_shape, jnp.float32),
        grid_spec=pltpu.PrefetchScalarGridSpec(
            num_scalar_prefetch=3,
            grid=(1,),
            in_specs=[
                pl.BlockSpec(memory_space=pl.ANY),
                pl.BlockSpec(dense.shape, lambda i, *_: (0,) * dense.ndim),
            ],
            out_specs=pl.BlockSpec(out_shape, lambda i, *_: (0,) * len(out_shape)),
            scratch_shapes=[
                pltpu.VMEM((2, GROUP, quarter, width), weights.dtype),
                pltpu.SemaphoreType.DMA((2, GROUP)),
            ],
        ),
    )(rows, members, slots, weights, dense)


def combine_apply(wanted, arrived, blocks_dev):
    slot_total, quarter, hidden = arrived.shape
    lines = slot_total // (CAP * X_SIZE * CORE_SIZE)
    return pl.pallas_call(
        combine_kernel,
        out_shape=jax.ShapeDtypeStruct((lines, blocks_dev, quarter, hidden), jnp.float32),
        grid_spec=pltpu.PrefetchScalarGridSpec(
            num_scalar_prefetch=1,
            grid=(1,),
            in_specs=[pl.BlockSpec(arrived.shape, lambda i, w: (0, 0, 0))],
            out_specs=pl.BlockSpec(
                (lines, blocks_dev, quarter, hidden), lambda i, w: (0, 0, 0, 0)
            ),
        ),
    )(wanted, arrived)


def grouping(row_ids, blocks_dev):
    block_count = row_ids.shape[0]
    group_count = block_count // GROUP + blocks_dev
    hot = (row_ids[:, None] == jnp.arange(blocks_dev, dtype=jnp.int32)[None, :]).astype(jnp.float32)
    block_range = jnp.arange(block_count, dtype=jnp.int32)
    before = (block_range[None, :] < block_range[:, None]).astype(jnp.float32)
    rank = jnp.sum(
        jnp.dot(before, hot, precision=lax.Precision.HIGHEST) * hot, axis=1
    ).astype(jnp.int32)
    counts = jnp.sum(hot, axis=0).astype(jnp.int32)
    groups_per_row = (counts + GROUP - 1) // GROUP
    group_end = jnp.cumsum(groups_per_row)
    group_start = group_end - groups_per_row
    position = jnp.sum(hot * group_start[None, :].astype(jnp.float32), axis=1).astype(jnp.int32) * GROUP + rank
    member = jnp.full((group_count * GROUP,), block_count, jnp.int32).at[position].set(block_range)
    group_range = jnp.arange(group_count, dtype=jnp.int32)
    group_row = jnp.minimum(
        jnp.sum((group_range[:, None] >= group_end[None, :]).astype(jnp.int32), axis=1), blocks_dev - 1
    ).astype(jnp.int32)
    return member, group_row


def per_device(teleport, cotangent, fetch_table, block_row, block_slot, values):
    row_count, hidden = teleport.shape
    quarter = values.shape[2]
    blocks_dev = row_count // quarter
    slot_total = fetch_table.shape[1]
    quarters = lax.axis_size("edge")
    row_peers = X_SIZE * CORE_SIZE
    z_me = lax.axis_index("z")
    x_me = lax.axis_index("x")
    c_me = lax.axis_index("c")
    weights = values[0]
    row_ids = block_row[0]
    slot_ids = block_slot[0]

    owner = slot_ids // CAP
    placed_slots = (
        ((owner // CORE_SIZE % X_SIZE * CORE_SIZE + owner % CORE_SIZE) * Z_SIZE + owner // (CORE_SIZE * X_SIZE))
        * CAP
        + slot_ids % CAP
    ).astype(jnp.int32)

    peer_range = jnp.arange(row_peers, dtype=jnp.int32)
    z_range = jnp.arange(Z_SIZE, dtype=jnp.int32)
    peer_groups = (z_me * X_SIZE + peer_range // CORE_SIZE) * CORE_SIZE + peer_range % CORE_SIZE
    line_owners = (z_range * X_SIZE + x_me) * CORE_SIZE + c_me
    table_cols = line_owners[:, None] * CAP + jnp.arange(CAP, dtype=jnp.int32)[None, :]
    wanted = fetch_table[peer_groups[:, None, None], table_cols[None, :, :]]
    send_index = (z_range[None, :, None] * blocks_dev + jnp.maximum(wanted, 0)).reshape(-1)

    member, group_row = grouping(row_ids, blocks_dev)
    member_slot = jnp.take(placed_slots, member, axis=0, mode="clip")
    wanted_flat = wanted.reshape(-1)

    current = teleport
    for step_index in range(STEPS):
        rounded = current.astype(jnp.bfloat16).reshape(blocks_dev, quarter, hidden)
        line_blocks = lax.all_gather(rounded, "z", axis=0, tiled=True)
        outgoing = jnp.take(line_blocks, send_index, axis=0)
        received = lax.all_to_all(
            outgoing, ("x", "c"), split_axis=0, concat_axis=0, tiled=True
        )
        partial = block_apply(
            forward_kernel, group_row, member, member_slot, weights, received,
            (quarters, blocks_dev, quarter, hidden),
        )
        summed = edge_exchange(partial, quarters, True, 1)
        current = 0.9 * summed.reshape(row_count, hidden) + 0.1 * teleport

    adjoint = cotangent
    gradient = 0.1 * cotangent
    for step_index in range(STEPS):
        rounded = adjoint.astype(jnp.bfloat16).reshape(1, blocks_dev, quarter, hidden)
        whole_rows = edge_exchange(rounded, quarters, False, 2)
        slot_sums = block_apply(
            backward_kernel, group_row, member, member_slot, weights, whole_rows,
            (slot_total, quarter, hidden),
        )
        arrived = lax.all_to_all(
            slot_sums, ("x", "c"), split_axis=0, concat_axis=0, tiled=True
        )
        dense = combine_apply(wanted_flat, arrived, blocks_dev)
        owned = lax.psum_scatter(dense, "z", scatter_dimension=0, tiled=True)
        adjoint = 0.9 * owned.reshape(row_count, hidden)
        factor = 0.1 if step_index + 1 < STEPS else 1.0
        gradient = gradient + factor * adjoint
    return (current, gradient)


def solution(mesh):
    devices = mesh.devices.reshape(Z_SIZE, X_SIZE, CORE_SIZE, mesh.shape["edge"])
    fine = Mesh(devices, ("z", "x", "c", "edge"))
    node = ("z", "x", "c")
    placed = (
        P((*node, "edge"), None),
        P((*node, "edge"), None),
        P(),
        P(node, None),
        P(node, None),
        P(node, None, "edge", None),
    )
    return jax.shard_map(
        per_device,
        mesh=fine,
        in_specs=placed,
        out_specs=(P((*node, "edge"), None), P((*node, "edge"), None)),
        check_vma=False,
    )
```

```python
import functools

import jax
import jax.numpy as jnp
from jax import lax
from jax.experimental import pallas as pl
from jax.experimental.pallas import tpu as pltpu
from jax.sharding import Mesh
from jax.sharding import PartitionSpec as P

MESH = pl.DeviceIdType.MESH

CAP = 2
STEPS = 2
Z_SIZE = 8
X_SIZE = 4
CORE_SIZE = 2
GROUP = 4


def fetch_all(members_ref, v_hbm, vbuf, sems):
    last = v_hbm.shape[0] - 1

    def issue(i, carry):
        b = jnp.minimum(members_ref[i], last)
        pltpu.make_async_copy(v_hbm.at[b], vbuf.at[i], sems.at[i]).start()
        return carry

    lax.fori_loop(0, vbuf.shape[0], issue, 0)


def wait_group(v_hbm, vbuf, sems, g):
    for m in range(GROUP):
        pltpu.make_async_copy(v_hbm.at[0], vbuf.at[g * GROUP + m], sems.at[g * GROUP + m]).wait()


def forward_kernel(rows_ref, members_ref, slots_ref, v_hbm, x_ref, out_ref, vbuf, sems):
    group_count = rows_ref.shape[0]
    block_count = v_hbm.shape[0]
    quarters, _, quarter, hidden = out_ref.shape
    fetch_all(members_ref, v_hbm, vbuf, sems)
    out_ref[...] = jnp.zeros_like(out_ref)

    def body(g, carry):
        wait_group(v_hbm, vbuf, sems, g)

        j = rows_ref[g]
        pieces = []
        for m in range(GROUP):
            valid = members_ref[g * GROUP + m] < block_count
            piece = x_ref[slots_ref[g * GROUP + m]]
            pieces.append(jnp.where(valid, piece, jnp.zeros_like(piece)))
        sources = jnp.concatenate(pieces, axis=0)
        weights = vbuf[pl.ds(g * GROUP, GROUP)].reshape(GROUP * quarter, vbuf.shape[-1])
        product = lax.dot_general(
            weights, sources, (((0,), (0,)), ((), ())), preferred_element_type=jnp.float32
        )
        out_ref[:, j] += product.reshape(quarters, quarter, hidden)
        return carry

    lax.fori_loop(0, group_count, body, 0)


def backward_kernel(rows_ref, members_ref, slots_ref, v_hbm, a_ref, out_ref, vbuf, sems):
    group_count = rows_ref.shape[0]
    block_count = v_hbm.shape[0]
    quarters, _, quarter, hidden = a_ref.shape
    fetch_all(members_ref, v_hbm, vbuf, sems)
    out_ref[...] = jnp.zeros_like(out_ref)

    def body(g, carry):
        wait_group(v_hbm, vbuf, sems, g)

        j = rows_ref[g]
        sources = a_ref[:, j].reshape(quarters * quarter, hidden)
        weights = vbuf[pl.ds(g * GROUP, GROUP)].reshape(GROUP * quarter, vbuf.shape[-1])
        product = jnp.dot(weights, sources, preferred_element_type=jnp.float32)
        for m in range(GROUP):
            s = slots_ref[g * GROUP + m]

            @pl.when(members_ref[g * GROUP + m] < block_count)
            def _():
                out_ref[s] += product[m * quarter:(m + 1) * quarter]

        return carry

    lax.fori_loop(0, group_count, body, 0)


def combine_kernel(want_ref, arrived_ref, out_ref):
    out_ref[...] = jnp.zeros_like(out_ref)
    lines = out_ref.shape[0]

    def body(q, carry):
        j = want_ref[q]

        @pl.when(j >= 0)
        def _():
            out_ref[q // CAP % lines, j] += arrived_ref[q]

        return carry

    lax.fori_loop(0, arrived_ref.shape[0], body, 0)


def edge_exchange_kernel(reduce, x_ref, out_ref, held, send_sem, recv_sem):
    count = held.shape[0]
    me = lax.axis_index("edge")
    barrier = pltpu.get_barrier_semaphore()
    for d in range(1, count):
        pl.semaphore_signal(
            barrier, inc=1, device_id={"edge": lax.rem(me + d, count)}, device_id_type=MESH
        )
    pl.semaphore_wait(barrier, count - 1)
    copies = []
    for d in range(1, count):
        peer = lax.rem(me + d, count)
        copy = pltpu.make_async_remote_copy(
            src_ref=x_ref.at[peer] if reduce else x_ref.at[0],
            dst_ref=held.at[me],
            send_sem=send_sem.at[d],
            recv_sem=recv_sem.at[d],
            device_id={"edge": peer},
            device_id_type=MESH,
        )
        copy.start()
        copies.append(copy)
    held[me] = x_ref[me] if reduce else x_ref[0]
    for copy in copies:
        copy.wait()
    if reduce:
        total = held[0]
        for q in range(1, count):
            total = total + held[q]
        out_ref[...] = total
    else:
        out_ref[...] = held[...]


def edge_exchange(chunks, count, reduce, collective_id):
    piece = chunks.shape[1:]
    out_shape = piece if reduce else (count,) + piece
    return pl.pallas_call(
        functools.partial(edge_exchange_kernel, reduce),
        out_shape=jax.ShapeDtypeStruct(out_shape, chunks.dtype),
        in_specs=[pl.BlockSpec(memory_space=pltpu.VMEM)],
        out_specs=pl.BlockSpec(memory_space=pltpu.VMEM),
        scratch_shapes=[
            pltpu.VMEM((count,) + piece, chunks.dtype),
            pltpu.SemaphoreType.DMA((count,)),
            pltpu.SemaphoreType.DMA((count,)),
        ],
        compiler_params=pltpu.CompilerParams(collective_id=collective_id, has_side_effects=True),
    )(chunks)


def block_apply(kernel, rows, members, slots, weights, dense, out_shape):
    block_count, quarter, width = weights.shape
    return pl.pallas_call(
        kernel,
        out_shape=jax.ShapeDtypeStruct(out_shape, jnp.float32),
        grid_spec=pltpu.PrefetchScalarGridSpec(
            num_scalar_prefetch=3,
            grid=(1,),
            in_specs=[
                pl.BlockSpec(memory_space=pl.ANY),
                pl.BlockSpec(dense.shape, lambda i, *_: (0,) * dense.ndim),
            ],
            out_specs=pl.BlockSpec(out_shape, lambda i, *_: (0,) * len(out_shape)),
            scratch_shapes=[
                pltpu.VMEM((members.shape[0], quarter, width), weights.dtype),
                pltpu.SemaphoreType.DMA((members.shape[0],)),
            ],
        ),
    )(rows, members, slots, weights, dense)


def combine_apply(wanted, arrived, blocks_dev):
    slot_total, quarter, hidden = arrived.shape
    lines = slot_total // (CAP * X_SIZE * CORE_SIZE)
    return pl.pallas_call(
        combine_kernel,
        out_shape=jax.ShapeDtypeStruct((lines, blocks_dev, quarter, hidden), jnp.float32),
        grid_spec=pltpu.PrefetchScalarGridSpec(
            num_scalar_prefetch=1,
            grid=(1,),
            in_specs=[pl.BlockSpec(arrived.shape, lambda i, w: (0, 0, 0))],
            out_specs=pl.BlockSpec(
                (lines, blocks_dev, quarter, hidden), lambda i, w: (0, 0, 0, 0)
            ),
        ),
    )(wanted, arrived)


def grouping(row_ids, blocks_dev):
    block_count = row_ids.shape[0]
    group_count = block_count // GROUP + blocks_dev
    hot = (row_ids[:, None] == jnp.arange(blocks_dev, dtype=jnp.int32)[None, :]).astype(jnp.float32)
    block_range = jnp.arange(block_count, dtype=jnp.int32)
    before = (block_range[None, :] < block_range[:, None]).astype(jnp.float32)
    rank = jnp.sum(
        jnp.dot(before, hot, precision=lax.Precision.HIGHEST) * hot, axis=1
    ).astype(jnp.int32)
    counts = jnp.sum(hot, axis=0).astype(jnp.int32)
    groups_per_row = (counts + GROUP - 1) // GROUP
    group_end = jnp.cumsum(groups_per_row)
    group_start = group_end - groups_per_row
    position = jnp.sum(hot * group_start[None, :].astype(jnp.float32), axis=1).astype(jnp.int32) * GROUP + rank
    member = jnp.full((group_count * GROUP,), block_count, jnp.int32).at[position].set(block_range)
    group_range = jnp.arange(group_count, dtype=jnp.int32)
    group_row = jnp.minimum(
        jnp.sum((group_range[:, None] >= group_end[None, :]).astype(jnp.int32), axis=1), blocks_dev - 1
    ).astype(jnp.int32)
    return member, group_row


def per_device(teleport, cotangent, fetch_table, block_row, block_slot, values):
    row_count, hidden = teleport.shape
    quarter = values.shape[2]
    blocks_dev = row_count // quarter
    slot_total = fetch_table.shape[1]
    quarters = lax.axis_size("edge")
    row_peers = X_SIZE * CORE_SIZE
    z_me = lax.axis_index("z")
    x_me = lax.axis_index("x")
    c_me = lax.axis_index("c")
    weights = values[0]
    row_ids = block_row[0]
    slot_ids = block_slot[0]

    owner = slot_ids // CAP
    placed_slots = (
        ((owner // CORE_SIZE % X_SIZE * CORE_SIZE + owner % CORE_SIZE) * Z_SIZE + owner // (CORE_SIZE * X_SIZE))
        * CAP
        + slot_ids % CAP
    ).astype(jnp.int32)

    peer_range = jnp.arange(row_peers, dtype=jnp.int32)
    z_range = jnp.arange(Z_SIZE, dtype=jnp.int32)
    peer_groups = (z_me * X_SIZE + peer_range // CORE_SIZE) * CORE_SIZE + peer_range % CORE_SIZE
    line_owners = (z_range * X_SIZE + x_me) * CORE_SIZE + c_me
    table_cols = line_owners[:, None] * CAP + jnp.arange(CAP, dtype=jnp.int32)[None, :]
    wanted = fetch_table[peer_groups[:, None, None], table_cols[None, :, :]]
    send_index = (z_range[None, :, None] * blocks_dev + jnp.maximum(wanted, 0)).reshape(-1)

    member, group_row = grouping(row_ids, blocks_dev)
    member_slot = jnp.take(placed_slots, member, axis=0, mode="clip")
    wanted_flat = wanted.reshape(-1)

    current = teleport
    for step_index in range(STEPS):
        rounded = current.astype(jnp.bfloat16).reshape(blocks_dev, quarter, hidden)
        line_blocks = lax.all_gather(rounded, "z", axis=0, tiled=True)
        outgoing = jnp.take(line_blocks, send_index, axis=0)
        received = lax.all_to_all(
            outgoing, ("x", "c"), split_axis=0, concat_axis=0, tiled=True
        )
        partial = block_apply(
            forward_kernel, group_row, member, member_slot, weights, received,
            (quarters, blocks_dev, quarter, hidden),
        )
        summed = edge_exchange(partial, quarters, True, 1)
        current = 0.9 * summed.reshape(row_count, hidden) + 0.1 * teleport

    adjoint = cotangent
    gradient = 0.1 * cotangent
    for step_index in range(STEPS):
        rounded = adjoint.astype(jnp.bfloat16).reshape(1, blocks_dev, quarter, hidden)
        whole_rows = edge_exchange(rounded, quarters, False, 2)
        slot_sums = block_apply(
            backward_kernel, group_row, member, member_slot, weights, whole_rows,
            (slot_total, quarter, hidden),
        )
        arrived = lax.all_to_all(
            slot_sums, ("x", "c"), split_axis=0, concat_axis=0, tiled=True
        )
        dense = combine_apply(wanted_flat, arrived, blocks_dev)
        owned = lax.psum_scatter(dense, "z", scatter_dimension=0, tiled=True)
        adjoint = 0.9 * owned.reshape(row_count, hidden)
        factor = 0.1 if step_index + 1 < STEPS else 1.0
        gradient = gradient + factor * adjoint
    return (current, gradient)


def solution(mesh):
    devices = mesh.devices.reshape(Z_SIZE, X_SIZE, CORE_SIZE, mesh.shape["edge"])
    fine = Mesh(devices, ("z", "x", "c", "edge"))
    node = ("z", "x", "c")
    placed = (
        P((*node, "edge"), None),
        P((*node, "edge"), None),
        P(),
        P(node, None),
        P(node, None),
        P(node, None, "edge", None),
    )
    return jax.shard_map(
        per_device,
        mesh=fine,
        in_specs=placed,
        out_specs=(P((*node, "edge"), None), P((*node, "edge"), None)),
        check_vma=False,
    )
```

```python
import functools

import jax
import jax.numpy as jnp
from jax import lax
from jax.experimental import pallas as pl
from jax.experimental.pallas import tpu as pltpu
from jax.sharding import Mesh
from jax.sharding import PartitionSpec as P

MESH = pl.DeviceIdType.MESH

CAP = 2
STEPS = 2
Z_SIZE = 8
X_SIZE = 4
CORE_SIZE = 2
GROUP = 4


def fetch_all(members_ref, v_hbm, vbuf, sems):
    last = v_hbm.shape[0] - 1

    def issue(i, carry):
        b = jnp.minimum(members_ref[i], last)
        pltpu.make_async_copy(v_hbm.at[b], vbuf.at[i], sems.at[i]).start()
        return carry

    lax.fori_loop(0, vbuf.shape[0], issue, 0)


def wait_group(v_hbm, vbuf, sems, g):
    for m in range(GROUP):
        pltpu.make_async_copy(v_hbm.at[0], vbuf.at[g * GROUP + m], sems.at[g * GROUP + m]).wait()


def forward_kernel(rows_ref, members_ref, slots_ref, v_hbm, x_ref, out_ref, vbuf, sems):
    group_count = rows_ref.shape[0]
    block_count = v_hbm.shape[0]
    quarters, _, quarter, hidden = out_ref.shape
    fetch_all(members_ref, v_hbm, vbuf, sems)
    out_ref[...] = jnp.zeros_like(out_ref)

    def body(g, carry):
        wait_group(v_hbm, vbuf, sems, g)

        j = rows_ref[g]
        pieces = []
        for m in range(GROUP):
            valid = members_ref[g * GROUP + m] < block_count
            piece = x_ref[slots_ref[g * GROUP + m]]
            pieces.append(jnp.where(valid, piece, jnp.zeros_like(piece)))
        sources = jnp.concatenate(pieces, axis=0)
        weights = vbuf[pl.ds(g * GROUP, GROUP)].reshape(GROUP * quarter, vbuf.shape[-1])
        product = lax.dot_general(
            weights, sources, (((0,), (0,)), ((), ())), preferred_element_type=jnp.float32
        )
        out_ref[:, j] += product.reshape(quarters, quarter, hidden)
        return carry

    lax.fori_loop(0, group_count, body, 0)


def backward_kernel(rows_ref, members_ref, slots_ref, v_hbm, a_ref, out_ref, vbuf, sems):
    group_count = rows_ref.shape[0]
    block_count = v_hbm.shape[0]
    quarters, _, quarter, hidden = a_ref.shape
    fetch_all(members_ref, v_hbm, vbuf, sems)
    out_ref[...] = jnp.zeros_like(out_ref)

    def body(g, carry):
        wait_group(v_hbm, vbuf, sems, g)

        j = rows_ref[g]
        sources = a_ref[:, j].reshape(quarters * quarter, hidden)
        weights = vbuf[pl.ds(g * GROUP, GROUP)].reshape(GROUP * quarter, vbuf.shape[-1])
        product = jnp.dot(weights, sources, preferred_element_type=jnp.float32)
        for m in range(GROUP):
            s = slots_ref[g * GROUP + m]

            @pl.when(members_ref[g * GROUP + m] < block_count)
            def _():
                out_ref[s] += product[m * quarter:(m + 1) * quarter]

        return carry

    lax.fori_loop(0, group_count, body, 0)


def combine_kernel(want_ref, arrived_ref, out_ref):
    out_ref[...] = jnp.zeros_like(out_ref)
    lines = out_ref.shape[0]

    def body(q, carry):
        j = want_ref[q]

        @pl.when(j >= 0)
        def _():
            out_ref[q // CAP % lines, j] += arrived_ref[q]

        return carry

    lax.fori_loop(0, arrived_ref.shape[0], body, 0)


def edge_exchange_kernel(reduce, x_ref, out_ref, held, send_sem, recv_sem):
    count = held.shape[0]
    me = lax.axis_index("edge")
    barrier = pltpu.get_barrier_semaphore()
    for d in range(1, count):
        pl.semaphore_signal(
            barrier, inc=1, device_id={"edge": lax.rem(me + d, count)}, device_id_type=MESH
        )
    pl.semaphore_wait(barrier, count - 1)
    copies = []
    for d in range(1, count):
        peer = lax.rem(me + d, count)
        copy = pltpu.make_async_remote_copy(
            src_ref=x_ref.at[peer] if reduce else x_ref.at[0],
            dst_ref=held.at[me],
            send_sem=send_sem.at[d],
            recv_sem=recv_sem.at[d],
            device_id={"edge": peer},
            device_id_type=MESH,
        )
        copy.start()
        copies.append(copy)
    held[me] = x_ref[me] if reduce else x_ref[0]
    for copy in copies:
        copy.wait()
    if reduce:
        total = held[0]
        for q in range(1, count):
            total = total + held[q]
        out_ref[...] = total
    else:
        out_ref[...] = held[...]


def edge_exchange(chunks, count, reduce, collective_id):
    piece = chunks.shape[1:]
    out_shape = piece if reduce else (count,) + piece
    return pl.pallas_call(
        functools.partial(edge_exchange_kernel, reduce),
        out_shape=jax.ShapeDtypeStruct(out_shape, chunks.dtype),
        in_specs=[pl.BlockSpec(memory_space=pltpu.VMEM)],
        out_specs=pl.BlockSpec(memory_space=pltpu.VMEM),
        scratch_shapes=[
            pltpu.VMEM((count,) + piece, chunks.dtype),
            pltpu.SemaphoreType.DMA((count,)),
            pltpu.SemaphoreType.DMA((count,)),
        ],
        compiler_params=pltpu.CompilerParams(collective_id=collective_id, has_side_effects=True),
    )(chunks)


def block_apply(kernel, rows, members, slots, weights, dense, out_shape):
    block_count, quarter, width = weights.shape
    return pl.pallas_call(
        kernel,
        out_shape=jax.ShapeDtypeStruct(out_shape, jnp.float32),
        grid_spec=pltpu.PrefetchScalarGridSpec(
            num_scalar_prefetch=3,
            grid=(1,),
            in_specs=[
                pl.BlockSpec(memory_space=pl.ANY),
                pl.BlockSpec(dense.shape, lambda i, *_: (0,) * dense.ndim),
            ],
            out_specs=pl.BlockSpec(out_shape, lambda i, *_: (0,) * len(out_shape)),
            scratch_shapes=[
                pltpu.VMEM((members.shape[0], quarter, width), weights.dtype),
                pltpu.SemaphoreType.DMA((members.shape[0],)),
            ],
        ),
    )(rows, members, slots, weights, dense)


def combine_apply(wanted, arrived, blocks_dev):
    slot_total, quarter, hidden = arrived.shape
    lines = slot_total // (CAP * X_SIZE * CORE_SIZE)
    return pl.pallas_call(
        combine_kernel,
        out_shape=jax.ShapeDtypeStruct((lines, blocks_dev, quarter, hidden), jnp.float32),
        grid_spec=pltpu.PrefetchScalarGridSpec(
            num_scalar_prefetch=1,
            grid=(1,),
            in_specs=[pl.BlockSpec(arrived.shape, lambda i, w: (0, 0, 0))],
            out_specs=pl.BlockSpec(
                (lines, blocks_dev, quarter, hidden), lambda i, w: (0, 0, 0, 0)
            ),
        ),
    )(wanted, arrived)


def grouping(row_ids, blocks_dev):
    block_count = row_ids.shape[0]
    group_count = block_count // GROUP + blocks_dev
    hot = (row_ids[:, None] == jnp.arange(blocks_dev, dtype=jnp.int32)[None, :]).astype(jnp.float32)
    block_range = jnp.arange(block_count, dtype=jnp.int32)
    before = (block_range[None, :] < block_range[:, None]).astype(jnp.float32)
    rank = jnp.sum(
        jnp.dot(before, hot, precision=lax.Precision.HIGHEST) * hot, axis=1
    ).astype(jnp.int32)
    counts = jnp.sum(hot, axis=0).astype(jnp.int32)
    groups_per_row = (counts + GROUP - 1) // GROUP
    group_end = jnp.cumsum(groups_per_row)
    group_start = group_end - groups_per_row
    position = jnp.sum(hot * group_start[None, :].astype(jnp.float32), axis=1).astype(jnp.int32) * GROUP + rank
    member = jnp.full((group_count * GROUP,), block_count, jnp.int32).at[position].set(block_range)
    group_range = jnp.arange(group_count, dtype=jnp.int32)
    group_row = jnp.minimum(
        jnp.sum((group_range[:, None] >= group_end[None, :]).astype(jnp.int32), axis=1), blocks_dev - 1
    ).astype(jnp.int32)
    return member, group_row


def per_device(teleport, cotangent, fetch_table, block_row, block_slot, values):
    row_count, hidden = teleport.shape
    quarter = values.shape[2]
    blocks_dev = row_count // quarter
    slot_total = fetch_table.shape[1]
    quarters = lax.axis_size("edge")
    row_peers = X_SIZE * CORE_SIZE
    z_me = lax.axis_index("z")
    x_me = lax.axis_index("x")
    c_me = lax.axis_index("c")
    weights = values[0]
    row_ids = block_row[0]
    slot_ids = block_slot[0]

    owner = slot_ids // CAP
    placed_slots = (
        ((owner // CORE_SIZE % X_SIZE * CORE_SIZE + owner % CORE_SIZE) * Z_SIZE + owner // (CORE_SIZE * X_SIZE))
        * CAP
        + slot_ids % CAP
    ).astype(jnp.int32)

    peer_range = jnp.arange(row_peers, dtype=jnp.int32)
    z_range = jnp.arange(Z_SIZE, dtype=jnp.int32)
    peer_groups = (z_me * X_SIZE + peer_range // CORE_SIZE) * CORE_SIZE + peer_range % CORE_SIZE
    line_owners = (z_range * X_SIZE + x_me) * CORE_SIZE + c_me
    table_cols = line_owners[:, None] * CAP + jnp.arange(CAP, dtype=jnp.int32)[None, :]
    wanted = fetch_table[peer_groups[:, None, None], table_cols[None, :, :]]
    me = (z_me * X_SIZE + x_me) * CORE_SIZE + c_me
    own_requests = lax.dynamic_slice_in_dim(fetch_table, me * CAP, CAP, 1).reshape(-1)
    send_index = jnp.maximum(own_requests, 0)

    member, group_row = grouping(row_ids, blocks_dev)
    member_slot = jnp.take(placed_slots, member, axis=0, mode="clip")
    reader_slot = jnp.take(slot_ids, member, axis=0, mode="clip")
    wanted_flat = wanted.reshape(-1)

    current = teleport
    for step_index in range(STEPS):
        rounded = current.astype(jnp.bfloat16).reshape(blocks_dev, quarter, hidden)
        outgoing = jnp.take(rounded, send_index, axis=0)
        received = lax.all_to_all(
            outgoing, ("z", "x", "c"), split_axis=0, concat_axis=0, tiled=True
        )
        partial = block_apply(
            forward_kernel, group_row, member, reader_slot, weights, received,
            (quarters, blocks_dev, quarter, hidden),
        )
        summed = edge_exchange(partial, quarters, True, 1)
        current = 0.9 * summed.reshape(row_count, hidden) + 0.1 * teleport

    adjoint = cotangent
    gradient = 0.1 * cotangent
    for step_index in range(STEPS):
        rounded = adjoint.astype(jnp.bfloat16).reshape(1, blocks_dev, quarter, hidden)
        whole_rows = edge_exchange(rounded, quarters, False, 2)
        slot_sums = block_apply(
            backward_kernel, group_row, member, member_slot, weights, whole_rows,
            (slot_total, quarter, hidden),
        )
        arrived = lax.all_to_all(
            slot_sums, ("x", "c"), split_axis=0, concat_axis=0, tiled=True
        )
        dense = combine_apply(wanted_flat, arrived, blocks_dev)
        owned = lax.psum_scatter(dense, "z", scatter_dimension=0, tiled=True)
        adjoint = 0.9 * owned.reshape(row_count, hidden)
        factor = 0.1 if step_index + 1 < STEPS else 1.0
        gradient = gradient + factor * adjoint
    return (current, gradient)


def solution(mesh):
    devices = mesh.devices.reshape(Z_SIZE, X_SIZE, CORE_SIZE, mesh.shape["edge"])
    fine = Mesh(devices, ("z", "x", "c", "edge"))
    node = ("z", "x", "c")
    placed = (
        P((*node, "edge"), None),
        P((*node, "edge"), None),
        P(),
        P(node, None),
        P(node, None),
        P(node, None, "edge", None),
    )
    return jax.shard_map(
        per_device,
        mesh=fine,
        in_specs=placed,
        out_specs=(P((*node, "edge"), None), P((*node, "edge"), None)),
        check_vma=False,
    )
```

```python
import functools

import jax
import jax.numpy as jnp
from jax import lax
from jax.experimental import pallas as pl
from jax.experimental.pallas import tpu as pltpu
from jax.sharding import Mesh
from jax.sharding import PartitionSpec as P

MESH = pl.DeviceIdType.MESH

CAP = 2
STEPS = 2
Z_SIZE = 8
X_SIZE = 4
CORE_SIZE = 2
GROUP = 4


def fetch_all(members_ref, v_hbm, vbuf, sems):
    last = v_hbm.shape[0] - 1

    def issue(i, carry):
        b = jnp.minimum(members_ref[i], last)
        pltpu.make_async_copy(v_hbm.at[b], vbuf.at[i], sems.at[i]).start()
        return carry

    lax.fori_loop(0, vbuf.shape[0], issue, 0, unroll=8)


def wait_group(v_hbm, vbuf, sems, g):
    for m in range(GROUP):
        pltpu.make_async_copy(v_hbm.at[0], vbuf.at[g * GROUP + m], sems.at[g * GROUP + m]).wait()


def forward_kernel(rows_ref, members_ref, slots_ref, v_hbm, x_ref, out_ref, vbuf, sems):
    group_count = rows_ref.shape[0]
    block_count = v_hbm.shape[0]
    quarters, _, quarter, hidden = out_ref.shape
    fetch_all(members_ref, v_hbm, vbuf, sems)
    out_ref[...] = jnp.zeros_like(out_ref)

    def body(g, carry):
        wait_group(v_hbm, vbuf, sems, g)

        j = rows_ref[g]
        pieces = []
        for m in range(GROUP):
            valid = members_ref[g * GROUP + m] < block_count
            piece = x_ref[slots_ref[g * GROUP + m]]
            pieces.append(jnp.where(valid, piece, jnp.zeros_like(piece)))
        sources = jnp.concatenate(pieces, axis=0)
        weights = vbuf[pl.ds(g * GROUP, GROUP)].reshape(GROUP * quarter, vbuf.shape[-1])
        product = lax.dot_general(
            weights, sources, (((0,), (0,)), ((), ())), preferred_element_type=jnp.float32
        )
        out_ref[:, j] += product.reshape(quarters, quarter, hidden)
        return carry

    lax.fori_loop(0, group_count, body, 0, unroll=4)


def backward_kernel(rows_ref, members_ref, slots_ref, v_hbm, a_ref, out_ref, vbuf, sems):
    group_count = rows_ref.shape[0]
    block_count = v_hbm.shape[0]
    quarters, _, quarter, hidden = a_ref.shape
    fetch_all(members_ref, v_hbm, vbuf, sems)
    out_ref[...] = jnp.zeros_like(out_ref)

    def body(g, carry):
        wait_group(v_hbm, vbuf, sems, g)

        j = rows_ref[g]
        sources = a_ref[:, j].reshape(quarters * quarter, hidden)
        weights = vbuf[pl.ds(g * GROUP, GROUP)].reshape(GROUP * quarter, vbuf.shape[-1])
        product = jnp.dot(weights, sources, preferred_element_type=jnp.float32)
        for m in range(GROUP):
            s = slots_ref[g * GROUP + m]

            @pl.when(members_ref[g * GROUP + m] < block_count)
            def _():
                out_ref[s] += product[m * quarter:(m + 1) * quarter]

        return carry

    lax.fori_loop(0, group_count, body, 0, unroll=4)


def combine_kernel(want_ref, arrived_ref, out_ref):
    out_ref[...] = jnp.zeros_like(out_ref)
    lines = out_ref.shape[0]

    def body(q, carry):
        j = want_ref[q]

        @pl.when(j >= 0)
        def _():
            out_ref[q // CAP % lines, j] += arrived_ref[q]

        return carry

    lax.fori_loop(0, arrived_ref.shape[0], body, 0, unroll=8)


def edge_exchange_kernel(reduce, x_ref, out_ref, held, send_sem, recv_sem):
    count = held.shape[0]
    me = lax.axis_index("edge")
    barrier = pltpu.get_barrier_semaphore()
    for d in range(1, count):
        pl.semaphore_signal(
            barrier, inc=1, device_id={"edge": lax.rem(me + d, count)}, device_id_type=MESH
        )
    pl.semaphore_wait(barrier, count - 1)
    copies = []
    for d in range(1, count):
        peer = lax.rem(me + d, count)
        copy = pltpu.make_async_remote_copy(
            src_ref=x_ref.at[peer] if reduce else x_ref.at[0],
            dst_ref=held.at[me],
            send_sem=send_sem.at[d],
            recv_sem=recv_sem.at[d],
            device_id={"edge": peer},
            device_id_type=MESH,
        )
        copy.start()
        copies.append(copy)
    held[me] = x_ref[me] if reduce else x_ref[0]
    for copy in copies:
        copy.wait()
    if reduce:
        total = held[0]
        for q in range(1, count):
            total = total + held[q]
        out_ref[...] = total
    else:
        out_ref[...] = held[...]


def edge_exchange(chunks, count, reduce, collective_id):
    piece = chunks.shape[1:]
    out_shape = piece if reduce else (count,) + piece
    return pl.pallas_call(
        functools.partial(edge_exchange_kernel, reduce),
        out_shape=jax.ShapeDtypeStruct(out_shape, chunks.dtype),
        in_specs=[pl.BlockSpec(memory_space=pltpu.VMEM)],
        out_specs=pl.BlockSpec(memory_space=pltpu.VMEM),
        scratch_shapes=[
            pltpu.VMEM((count,) + piece, chunks.dtype),
            pltpu.SemaphoreType.DMA((count,)),
            pltpu.SemaphoreType.DMA((count,)),
        ],
        compiler_params=pltpu.CompilerParams(collective_id=collective_id, has_side_effects=True),
    )(chunks)


def block_apply(kernel, rows, members, slots, weights, dense, out_shape):
    block_count, quarter, width = weights.shape
    return pl.pallas_call(
        kernel,
        out_shape=jax.ShapeDtypeStruct(out_shape, jnp.float32),
        grid_spec=pltpu.PrefetchScalarGridSpec(
            num_scalar_prefetch=3,
            grid=(1,),
            in_specs=[
                pl.BlockSpec(memory_space=pl.ANY),
                pl.BlockSpec(dense.shape, lambda i, *_: (0,) * dense.ndim),
            ],
            out_specs=pl.BlockSpec(out_shape, lambda i, *_: (0,) * len(out_shape)),
            scratch_shapes=[
                pltpu.VMEM((members.shape[0], quarter, width), weights.dtype),
                pltpu.SemaphoreType.DMA((members.shape[0],)),
            ],
        ),
    )(rows, members, slots, weights, dense)


def combine_apply(wanted, arrived, blocks_dev):
    slot_total, quarter, hidden = arrived.shape
    lines = slot_total // (CAP * X_SIZE * CORE_SIZE)
    return pl.pallas_call(
        combine_kernel,
        out_shape=jax.ShapeDtypeStruct((lines, blocks_dev, quarter, hidden), jnp.float32),
        grid_spec=pltpu.PrefetchScalarGridSpec(
            num_scalar_prefetch=1,
            grid=(1,),
            in_specs=[pl.BlockSpec(arrived.shape, lambda i, w: (0, 0, 0))],
            out_specs=pl.BlockSpec(
                (lines, blocks_dev, quarter, hidden), lambda i, w: (0, 0, 0, 0)
            ),
        ),
    )(wanted, arrived)


def grouping(row_ids, blocks_dev):
    block_count = row_ids.shape[0]
    group_count = block_count // GROUP + blocks_dev
    hot = (row_ids[:, None] == jnp.arange(blocks_dev, dtype=jnp.int32)[None, :]).astype(jnp.float32)
    block_range = jnp.arange(block_count, dtype=jnp.int32)
    before = (block_range[None, :] < block_range[:, None]).astype(jnp.float32)
    rank = jnp.sum(
        jnp.dot(before, hot, precision=lax.Precision.HIGHEST) * hot, axis=1
    ).astype(jnp.int32)
    counts = jnp.sum(hot, axis=0).astype(jnp.int32)
    groups_per_row = (counts + GROUP - 1) // GROUP
    group_end = jnp.cumsum(groups_per_row)
    group_start = group_end - groups_per_row
    position = jnp.sum(hot * group_start[None, :].astype(jnp.float32), axis=1).astype(jnp.int32) * GROUP + rank
    member = jnp.full((group_count * GROUP,), block_count, jnp.int32).at[position].set(block_range)
    group_range = jnp.arange(group_count, dtype=jnp.int32)
    group_row = jnp.minimum(
        jnp.sum((group_range[:, None] >= group_end[None, :]).astype(jnp.int32), axis=1), blocks_dev - 1
    ).astype(jnp.int32)
    return member, group_row


def per_device(teleport, cotangent, fetch_table, block_row, block_slot, values):
    row_count, hidden = teleport.shape
    quarter = values.shape[2]
    blocks_dev = row_count // quarter
    slot_total = fetch_table.shape[1]
    quarters = lax.axis_size("edge")
    row_peers = X_SIZE * CORE_SIZE
    z_me = lax.axis_index("z")
    x_me = lax.axis_index("x")
    c_me = lax.axis_index("c")
    weights = values[0]
    row_ids = block_row[0]
    slot_ids = block_slot[0]

    owner = slot_ids // CAP
    placed_slots = (
        ((owner // CORE_SIZE % X_SIZE * CORE_SIZE + owner % CORE_SIZE) * Z_SIZE + owner // (CORE_SIZE * X_SIZE))
        * CAP
        + slot_ids % CAP
    ).astype(jnp.int32)

    peer_range = jnp.arange(row_peers, dtype=jnp.int32)
    z_range = jnp.arange(Z_SIZE, dtype=jnp.int32)
    peer_groups = (z_me * X_SIZE + peer_range // CORE_SIZE) * CORE_SIZE + peer_range % CORE_SIZE
    line_owners = (z_range * X_SIZE + x_me) * CORE_SIZE + c_me
    table_cols = line_owners[:, None] * CAP + jnp.arange(CAP, dtype=jnp.int32)[None, :]
    wanted = fetch_table[peer_groups[:, None, None], table_cols[None, :, :]]
    send_index = (z_range[None, :, None] * blocks_dev + jnp.maximum(wanted, 0)).reshape(-1)

    member, group_row = grouping(row_ids, blocks_dev)
    member_slot = jnp.take(placed_slots, member, axis=0, mode="clip")
    wanted_flat = wanted.reshape(-1)

    current = teleport
    for step_index in range(STEPS):
        rounded = current.astype(jnp.bfloat16).reshape(blocks_dev, quarter, hidden)
        line_blocks = lax.all_gather(rounded, "z", axis=0, tiled=True)
        outgoing = jnp.take(line_blocks, send_index, axis=0)
        received = lax.all_to_all(
            outgoing, ("x", "c"), split_axis=0, concat_axis=0, tiled=True
        )
        partial = block_apply(
            forward_kernel, group_row, member, member_slot, weights, received,
            (quarters, blocks_dev, quarter, hidden),
        )
        summed = edge_exchange(partial, quarters, True, 1)
        current = 0.9 * summed.reshape(row_count, hidden) + 0.1 * teleport

    adjoint = cotangent
    gradient = 0.1 * cotangent
    for step_index in range(STEPS):
        rounded = adjoint.astype(jnp.bfloat16).reshape(1, blocks_dev, quarter, hidden)
        whole_rows = edge_exchange(rounded, quarters, False, 2)
        slot_sums = block_apply(
            backward_kernel, group_row, member, member_slot, weights, whole_rows,
            (slot_total, quarter, hidden),
        )
        arrived = lax.all_to_all(
            slot_sums, ("x", "c"), split_axis=0, concat_axis=0, tiled=True
        )
        dense = combine_apply(wanted_flat, arrived, blocks_dev)
        owned = lax.psum_scatter(dense, "z", scatter_dimension=0, tiled=True)
        adjoint = 0.9 * owned.reshape(row_count, hidden)
        factor = 0.1 if step_index + 1 < STEPS else 1.0
        gradient = gradient + factor * adjoint
    return (current, gradient)


def solution(mesh):
    devices = mesh.devices.reshape(Z_SIZE, X_SIZE, CORE_SIZE, mesh.shape["edge"])
    fine = Mesh(devices, ("z", "x", "c", "edge"))
    node = ("z", "x", "c")
    placed = (
        P((*node, "edge"), None),
        P((*node, "edge"), None),
        P(),
        P(node, None),
        P(node, None),
        P(node, None, "edge", None),
    )
    return jax.shard_map(
        per_device,
        mesh=fine,
        in_specs=placed,
        out_specs=(P((*node, "edge"), None), P((*node, "edge"), None)),
        check_vma=False,
    )
```

```python
import functools

import jax
import jax.numpy as jnp
from jax import lax
from jax.experimental import pallas as pl
from jax.experimental.pallas import tpu as pltpu
from jax.sharding import Mesh
from jax.sharding import PartitionSpec as P

MESH = pl.DeviceIdType.MESH

CAP = 2
STEPS = 2
Z_SIZE = 8
X_SIZE = 4
CORE_SIZE = 2
GROUP = 4


def fetch_all(members_ref, v_hbm, vbuf, sems):
    last = v_hbm.shape[0] - 1

    def issue(i, carry):
        b = jnp.minimum(members_ref[i], last)
        pltpu.make_async_copy(v_hbm.at[b], vbuf.at[i], sems.at[i]).start()
        return carry

    lax.fori_loop(0, vbuf.shape[0], issue, 0, unroll=8)


def wait_group(v_hbm, vbuf, sems, g):
    for m in range(GROUP):
        pltpu.make_async_copy(v_hbm.at[0], vbuf.at[g * GROUP + m], sems.at[g * GROUP + m]).wait()


def forward_kernel(rows_ref, members_ref, slots_ref, v_hbm, x_ref, out_ref, vbuf, sems):
    group_count = rows_ref.shape[0]
    block_count = v_hbm.shape[0]
    quarters, _, quarter, hidden = out_ref.shape
    fetch_all(members_ref, v_hbm, vbuf, sems)
    out_ref[...] = jnp.zeros_like(out_ref)

    def body(g, carry):
        wait_group(v_hbm, vbuf, sems, g)

        j = rows_ref[g]
        pieces = []
        for m in range(GROUP):
            valid = members_ref[g * GROUP + m] < block_count
            piece = x_ref[slots_ref[g * GROUP + m]]
            pieces.append(jnp.where(valid, piece, jnp.zeros_like(piece)))
        sources = jnp.concatenate(pieces, axis=0)
        weights = vbuf[pl.ds(g * GROUP, GROUP)].reshape(GROUP * quarter, vbuf.shape[-1])
        product = lax.dot_general(
            weights, sources, (((0,), (0,)), ((), ())), preferred_element_type=jnp.float32
        )
        out_ref[:, j] += product.reshape(quarters, quarter, hidden)
        return carry

    lax.fori_loop(0, group_count, body, 0, unroll=4)


def backward_kernel(rows_ref, members_ref, slots_ref, v_hbm, a_ref, out_ref, vbuf, sems):
    group_count = rows_ref.shape[0]
    block_count = v_hbm.shape[0]
    quarters, _, quarter, hidden = a_ref.shape
    fetch_all(members_ref, v_hbm, vbuf, sems)
    out_ref[...] = jnp.zeros_like(out_ref)

    def body(g, carry):
        wait_group(v_hbm, vbuf, sems, g)

        j = rows_ref[g]
        sources = a_ref[:, j].reshape(quarters * quarter, hidden)
        weights = vbuf[pl.ds(g * GROUP, GROUP)].reshape(GROUP * quarter, vbuf.shape[-1])
        product = jnp.dot(weights, sources, preferred_element_type=jnp.float32)
        for m in range(GROUP):
            s = slots_ref[g * GROUP + m]

            @pl.when(members_ref[g * GROUP + m] < block_count)
            def _():
                out_ref[s] += product[m * quarter:(m + 1) * quarter]

        return carry

    lax.fori_loop(0, group_count, body, 0, unroll=4)


def combine_kernel(want_ref, arrived_ref, out_ref):
    out_ref[...] = jnp.zeros_like(out_ref)
    lines = out_ref.shape[0]

    def body(q, carry):
        j = want_ref[q]

        @pl.when(j >= 0)
        def _():
            out_ref[q // CAP % lines, j] += arrived_ref[q]

        return carry

    lax.fori_loop(0, arrived_ref.shape[0], body, 0, unroll=8)


def edge_exchange_kernel(reduce, x_ref, out_ref, held, send_sem, recv_sem):
    count = held.shape[0]
    me = lax.axis_index("edge")
    barrier = pltpu.get_barrier_semaphore()
    for d in range(1, count):
        pl.semaphore_signal(
            barrier, inc=1, device_id={"edge": lax.rem(me + d, count)}, device_id_type=MESH
        )
    pl.semaphore_wait(barrier, count - 1)
    copies = []
    for d in range(1, count):
        peer = lax.rem(me + d, count)
        copy = pltpu.make_async_remote_copy(
            src_ref=x_ref.at[peer] if reduce else x_ref.at[0],
            dst_ref=held.at[me],
            send_sem=send_sem.at[d],
            recv_sem=recv_sem.at[d],
            device_id={"edge": peer},
            device_id_type=MESH,
        )
        copy.start()
        copies.append(copy)
    held[me] = x_ref[me] if reduce else x_ref[0]
    for copy in copies:
        copy.wait()
    if reduce:
        total = held[0]
        for q in range(1, count):
            total = total + held[q]
        out_ref[...] = total
    else:
        out_ref[...] = held[...]


def edge_exchange(chunks, count, reduce, collective_id):
    piece = chunks.shape[1:]
    out_shape = piece if reduce else (count,) + piece
    return pl.pallas_call(
        functools.partial(edge_exchange_kernel, reduce),
        out_shape=jax.ShapeDtypeStruct(out_shape, chunks.dtype),
        in_specs=[pl.BlockSpec(memory_space=pltpu.VMEM)],
        out_specs=pl.BlockSpec(memory_space=pltpu.VMEM),
        scratch_shapes=[
            pltpu.VMEM((count,) + piece, chunks.dtype),
            pltpu.SemaphoreType.DMA((count,)),
            pltpu.SemaphoreType.DMA((count,)),
        ],
        compiler_params=pltpu.CompilerParams(collective_id=collective_id, has_side_effects=True),
    )(chunks)


def block_apply(kernel, rows, members, slots, weights, dense, out_shape):
    block_count, quarter, width = weights.shape
    return pl.pallas_call(
        kernel,
        out_shape=jax.ShapeDtypeStruct(out_shape, jnp.float32),
        grid_spec=pltpu.PrefetchScalarGridSpec(
            num_scalar_prefetch=3,
            grid=(1,),
            in_specs=[
                pl.BlockSpec(memory_space=pl.ANY),
                pl.BlockSpec(dense.shape, lambda i, *_: (0,) * dense.ndim),
            ],
            out_specs=pl.BlockSpec(out_shape, lambda i, *_: (0,) * len(out_shape)),
            scratch_shapes=[
                pltpu.VMEM((members.shape[0], quarter, width), weights.dtype),
                pltpu.SemaphoreType.DMA((members.shape[0],)),
            ],
        ),
    )(rows, members, slots, weights, dense)


def combine_apply(wanted, arrived, blocks_dev):
    slot_total, quarter, hidden = arrived.shape
    lines = slot_total // (CAP * X_SIZE * CORE_SIZE)
    return pl.pallas_call(
        combine_kernel,
        out_shape=jax.ShapeDtypeStruct((lines, blocks_dev, quarter, hidden), jnp.float32),
        grid_spec=pltpu.PrefetchScalarGridSpec(
            num_scalar_prefetch=1,
            grid=(1,),
            in_specs=[pl.BlockSpec(arrived.shape, lambda i, w: (0, 0, 0))],
            out_specs=pl.BlockSpec(
                (lines, blocks_dev, quarter, hidden), lambda i, w: (0, 0, 0, 0)
            ),
        ),
    )(wanted, arrived)


def grouping(row_ids, blocks_dev):
    block_count = row_ids.shape[0]
    group_count = block_count // GROUP + blocks_dev
    hot = (row_ids[:, None] == jnp.arange(blocks_dev, dtype=jnp.int32)[None, :]).astype(jnp.float32)
    block_range = jnp.arange(block_count, dtype=jnp.int32)
    before = (block_range[None, :] < block_range[:, None]).astype(jnp.float32)
    rank = jnp.sum(
        jnp.dot(before, hot, precision=lax.Precision.HIGHEST) * hot, axis=1
    ).astype(jnp.int32)
    counts = jnp.sum(hot, axis=0).astype(jnp.int32)
    groups_per_row = (counts + GROUP - 1) // GROUP
    group_end = jnp.cumsum(groups_per_row)
    group_start = group_end - groups_per_row
    position = jnp.sum(hot * group_start[None, :].astype(jnp.float32), axis=1).astype(jnp.int32) * GROUP + rank
    member = jnp.full((group_count * GROUP,), block_count, jnp.int32).at[position].set(block_range)
    group_range = jnp.arange(group_count, dtype=jnp.int32)
    group_row = jnp.minimum(
        jnp.sum((group_range[:, None] >= group_end[None, :]).astype(jnp.int32), axis=1), blocks_dev - 1
    ).astype(jnp.int32)
    return member, group_row


def per_device(teleport, cotangent, fetch_table, block_row, block_slot, values):
    row_count, hidden = teleport.shape
    quarter = values.shape[2]
    blocks_dev = row_count // quarter
    slot_total = fetch_table.shape[1]
    quarters = lax.axis_size("edge")
    row_peers = X_SIZE * CORE_SIZE
    z_me = lax.axis_index("z")
    x_me = lax.axis_index("x")
    c_me = lax.axis_index("c")
    weights = values[0]
    row_ids = block_row[0]
    slot_ids = block_slot[0]

    owner = slot_ids // CAP
    placed_slots = (
        ((owner // CORE_SIZE % X_SIZE * CORE_SIZE + owner % CORE_SIZE) * Z_SIZE + owner // (CORE_SIZE * X_SIZE))
        * CAP
        + slot_ids % CAP
    ).astype(jnp.int32)

    peer_range = jnp.arange(row_peers, dtype=jnp.int32)
    z_range = jnp.arange(Z_SIZE, dtype=jnp.int32)
    peer_groups = (z_me * X_SIZE + peer_range // CORE_SIZE) * CORE_SIZE + peer_range % CORE_SIZE
    line_owners = (z_range * X_SIZE + x_me) * CORE_SIZE + c_me
    table_cols = line_owners[:, None] * CAP + jnp.arange(CAP, dtype=jnp.int32)[None, :]
    wanted = fetch_table[peer_groups[:, None, None], table_cols[None, :, :]]
    send_index = (z_range[None, :, None] * blocks_dev + jnp.maximum(wanted, 0)).reshape(-1)

    member, group_row = grouping(row_ids, blocks_dev)
    member_slot = jnp.take(placed_slots, member, axis=0, mode="clip")
    wanted_flat = wanted.reshape(-1)

    current = teleport
    adjoint = cotangent
    gradient = 0.1 * cotangent
    for step_index in range(STEPS):
        rounded = current.astype(jnp.bfloat16).reshape(blocks_dev, quarter, hidden)
        line_blocks = lax.all_gather(rounded, "z", axis=0, tiled=True)
        outgoing = jnp.take(line_blocks, send_index, axis=0)
        received = lax.all_to_all(
            outgoing, ("x", "c"), split_axis=0, concat_axis=0, tiled=True
        )
        partial = block_apply(
            forward_kernel, group_row, member, member_slot, weights, received,
            (quarters, blocks_dev, quarter, hidden),
        )
        summed = edge_exchange(partial, quarters, True, 1)
        current = 0.9 * summed.reshape(row_count, hidden) + 0.1 * teleport

        rounded = adjoint.astype(jnp.bfloat16).reshape(1, blocks_dev, quarter, hidden)
        whole_rows = edge_exchange(rounded, quarters, False, 2)
        slot_sums = block_apply(
            backward_kernel, group_row, member, member_slot, weights, whole_rows,
            (slot_total, quarter, hidden),
        )
        arrived = lax.all_to_all(
            slot_sums, ("x", "c"), split_axis=0, concat_axis=0, tiled=True
        )
        dense = combine_apply(wanted_flat, arrived, blocks_dev)
        owned = lax.psum_scatter(dense, "z", scatter_dimension=0, tiled=True)
        adjoint = 0.9 * owned.reshape(row_count, hidden)
        factor = 0.1 if step_index + 1 < STEPS else 1.0
        gradient = gradient + factor * adjoint
        if step_index + 1 < STEPS:
            current, adjoint = lax.optimization_barrier((current, adjoint))
    return (current, gradient)


def solution(mesh):
    devices = mesh.devices.reshape(Z_SIZE, X_SIZE, CORE_SIZE, mesh.shape["edge"])
    fine = Mesh(devices, ("z", "x", "c", "edge"))
    node = ("z", "x", "c")
    placed = (
        P((*node, "edge"), None),
        P((*node, "edge"), None),
        P(),
        P(node, None),
        P(node, None),
        P(node, None, "edge", None),
    )
    return jax.shard_map(
        per_device,
        mesh=fine,
        in_specs=placed,
        out_specs=(P((*node, "edge"), None), P((*node, "edge"), None)),
        check_vma=False,
    )
```

```python
import functools

import jax
import jax.numpy as jnp
from jax import lax
from jax.experimental import pallas as pl
from jax.experimental.pallas import tpu as pltpu
from jax.sharding import Mesh
from jax.sharding import PartitionSpec as P

MESH = pl.DeviceIdType.MESH

CAP = 2
STEPS = 2
Z_SIZE = 8
X_SIZE = 4
CORE_SIZE = 2
GROUP = 4
GROUPS_PER_STEP = 8
BLOCKS = 192


def forward_kernel(rows_ref, members_ref, slots_ref, v_ref, x_ref, out_ref):
    block_count = BLOCKS
    step = pl.program_id(0)
    quarters, _, quarter, hidden = out_ref.shape

    @pl.when(step == 0)
    def _():
        out_ref[...] = jnp.zeros_like(out_ref)

    def body(i, carry):
        g = step * GROUPS_PER_STEP + i

        j = rows_ref[g]
        pieces = []
        for m in range(GROUP):
            valid = members_ref[g * GROUP + m] < block_count
            piece = x_ref[slots_ref[g * GROUP + m]]
            pieces.append(jnp.where(valid, piece, jnp.zeros_like(piece)))
        sources = jnp.concatenate(pieces, axis=0)
        weights = v_ref[i]
        product = lax.dot_general(
            weights, sources, (((0,), (0,)), ((), ())), preferred_element_type=jnp.float32
        )
        out_ref[:, j] += product.reshape(quarters, quarter, hidden)
        return carry

    lax.fori_loop(0, GROUPS_PER_STEP, body, 0, unroll=4)


def backward_kernel(rows_ref, members_ref, slots_ref, v_ref, a_ref, out_ref):
    block_count = BLOCKS
    step = pl.program_id(0)
    quarters, _, quarter, hidden = a_ref.shape

    @pl.when(step == 0)
    def _():
        out_ref[...] = jnp.zeros_like(out_ref)

    def body(i, carry):
        g = step * GROUPS_PER_STEP + i

        j = rows_ref[g]
        sources = a_ref[:, j].reshape(quarters * quarter, hidden)
        weights = v_ref[i]
        product = jnp.dot(weights, sources, preferred_element_type=jnp.float32)
        for m in range(GROUP):
            s = slots_ref[g * GROUP + m]

            @pl.when(members_ref[g * GROUP + m] < block_count)
            def _():
                out_ref[s] += product[m * quarter:(m + 1) * quarter]

        return carry

    lax.fori_loop(0, GROUPS_PER_STEP, body, 0, unroll=4)


def combine_kernel(want_ref, arrived_ref, out_ref):
    out_ref[...] = jnp.zeros_like(out_ref)
    lines = out_ref.shape[0]

    def body(q, carry):
        j = want_ref[q]

        @pl.when(j >= 0)
        def _():
            out_ref[q // CAP % lines, j] += arrived_ref[q]

        return carry

    lax.fori_loop(0, arrived_ref.shape[0], body, 0, unroll=8)


def edge_exchange_kernel(reduce, x_ref, out_ref, held, send_sem, recv_sem):
    count = held.shape[0]
    me = lax.axis_index("edge")
    barrier = pltpu.get_barrier_semaphore()
    for d in range(1, count):
        pl.semaphore_signal(
            barrier, inc=1, device_id={"edge": lax.rem(me + d, count)}, device_id_type=MESH
        )
    pl.semaphore_wait(barrier, count - 1)
    copies = []
    for d in range(1, count):
        peer = lax.rem(me + d, count)
        copy = pltpu.make_async_remote_copy(
            src_ref=x_ref.at[peer] if reduce else x_ref.at[0],
            dst_ref=held.at[me],
            send_sem=send_sem.at[d],
            recv_sem=recv_sem.at[d],
            device_id={"edge": peer},
            device_id_type=MESH,
        )
        copy.start()
        copies.append(copy)
    held[me] = x_ref[me] if reduce else x_ref[0]
    for copy in copies:
        copy.wait()
    if reduce:
        total = held[0]
        for q in range(1, count):
            total = total + held[q]
        out_ref[...] = total
    else:
        out_ref[...] = held[...]


def edge_exchange(chunks, count, reduce, collective_id):
    piece = chunks.shape[1:]
    out_shape = piece if reduce else (count,) + piece
    return pl.pallas_call(
        functools.partial(edge_exchange_kernel, reduce),
        out_shape=jax.ShapeDtypeStruct(out_shape, chunks.dtype),
        in_specs=[pl.BlockSpec(memory_space=pltpu.VMEM)],
        out_specs=pl.BlockSpec(memory_space=pltpu.VMEM),
        scratch_shapes=[
            pltpu.VMEM((count,) + piece, chunks.dtype),
            pltpu.SemaphoreType.DMA((count,)),
            pltpu.SemaphoreType.DMA((count,)),
        ],
        compiler_params=pltpu.CompilerParams(collective_id=collective_id, has_side_effects=True),
    )(chunks)


def block_apply(kernel, rows, members, slots, weights_g, dense, out_shape):
    group_count, depth, width = weights_g.shape
    return pl.pallas_call(
        kernel,
        out_shape=jax.ShapeDtypeStruct(out_shape, jnp.float32),
        grid_spec=pltpu.PrefetchScalarGridSpec(
            num_scalar_prefetch=3,
            grid=(group_count // GROUPS_PER_STEP,),
            in_specs=[
                pl.BlockSpec((GROUPS_PER_STEP, depth, width), lambda i, *_: (i, 0, 0)),
                pl.BlockSpec(dense.shape, lambda i, *_: (0,) * dense.ndim),
            ],
            out_specs=pl.BlockSpec(out_shape, lambda i, *_: (0,) * len(out_shape)),
        ),
        compiler_params=pltpu.CompilerParams(dimension_semantics=("arbitrary",)),
    )(rows, members, slots, weights_g, dense)


def combine_apply(wanted, arrived, blocks_dev):
    slot_total, quarter, hidden = arrived.shape
    lines = slot_total // (CAP * X_SIZE * CORE_SIZE)
    return pl.pallas_call(
        combine_kernel,
        out_shape=jax.ShapeDtypeStruct((lines, blocks_dev, quarter, hidden), jnp.float32),
        grid_spec=pltpu.PrefetchScalarGridSpec(
            num_scalar_prefetch=1,
            grid=(1,),
            in_specs=[pl.BlockSpec(arrived.shape, lambda i, w: (0, 0, 0))],
            out_specs=pl.BlockSpec(
                (lines, blocks_dev, quarter, hidden), lambda i, w: (0, 0, 0, 0)
            ),
        ),
    )(wanted, arrived)


def grouping(row_ids, blocks_dev):
    block_count = row_ids.shape[0]
    group_count = block_count // GROUP + blocks_dev
    hot = (row_ids[:, None] == jnp.arange(blocks_dev, dtype=jnp.int32)[None, :]).astype(jnp.float32)
    block_range = jnp.arange(block_count, dtype=jnp.int32)
    before = (block_range[None, :] < block_range[:, None]).astype(jnp.float32)
    rank = jnp.sum(
        jnp.dot(before, hot, precision=lax.Precision.HIGHEST) * hot, axis=1
    ).astype(jnp.int32)
    counts = jnp.sum(hot, axis=0).astype(jnp.int32)
    groups_per_row = (counts + GROUP - 1) // GROUP
    group_end = jnp.cumsum(groups_per_row)
    group_start = group_end - groups_per_row
    position = jnp.sum(hot * group_start[None, :].astype(jnp.float32), axis=1).astype(jnp.int32) * GROUP + rank
    member = jnp.full((group_count * GROUP,), block_count, jnp.int32).at[position].set(block_range)
    group_range = jnp.arange(group_count, dtype=jnp.int32)
    group_row = jnp.minimum(
        jnp.sum((group_range[:, None] >= group_end[None, :]).astype(jnp.int32), axis=1), blocks_dev - 1
    ).astype(jnp.int32)
    return member, group_row


def per_device(teleport, cotangent, fetch_table, block_row, block_slot, values):
    row_count, hidden = teleport.shape
    quarter = values.shape[2]
    blocks_dev = row_count // quarter
    slot_total = fetch_table.shape[1]
    quarters = lax.axis_size("edge")
    row_peers = X_SIZE * CORE_SIZE
    z_me = lax.axis_index("z")
    x_me = lax.axis_index("x")
    c_me = lax.axis_index("c")
    weights = values[0]
    row_ids = block_row[0]
    slot_ids = block_slot[0]

    owner = slot_ids // CAP
    placed_slots = (
        ((owner // CORE_SIZE % X_SIZE * CORE_SIZE + owner % CORE_SIZE) * Z_SIZE + owner // (CORE_SIZE * X_SIZE))
        * CAP
        + slot_ids % CAP
    ).astype(jnp.int32)

    peer_range = jnp.arange(row_peers, dtype=jnp.int32)
    z_range = jnp.arange(Z_SIZE, dtype=jnp.int32)
    peer_groups = (z_me * X_SIZE + peer_range // CORE_SIZE) * CORE_SIZE + peer_range % CORE_SIZE
    line_owners = (z_range * X_SIZE + x_me) * CORE_SIZE + c_me
    table_cols = line_owners[:, None] * CAP + jnp.arange(CAP, dtype=jnp.int32)[None, :]
    wanted = fetch_table[peer_groups[:, None, None], table_cols[None, :, :]]
    send_index = (z_range[None, :, None] * blocks_dev + jnp.maximum(wanted, 0)).reshape(-1)

    member, group_row = grouping(row_ids, blocks_dev)
    member_slot = jnp.take(placed_slots, member, axis=0, mode="clip")
    weights_g = jnp.take(weights, member, axis=0, mode="clip").reshape(
        member.shape[0] // GROUP, GROUP * quarter, weights.shape[2]
    )
    wanted_flat = wanted.reshape(-1)

    current = teleport
    for step_index in range(STEPS):
        rounded = current.astype(jnp.bfloat16).reshape(blocks_dev, quarter, hidden)
        line_blocks = lax.all_gather(rounded, "z", axis=0, tiled=True)
        outgoing = jnp.take(line_blocks, send_index, axis=0)
        received = lax.all_to_all(
            outgoing, ("x", "c"), split_axis=0, concat_axis=0, tiled=True
        )
        partial = block_apply(
            forward_kernel, group_row, member, member_slot, weights_g, received,
            (quarters, blocks_dev, quarter, hidden),
        )
        summed = edge_exchange(partial, quarters, True, 1)
        current = 0.9 * summed.reshape(row_count, hidden) + 0.1 * teleport

    adjoint = cotangent
    gradient = 0.1 * cotangent
    for step_index in range(STEPS):
        rounded = adjoint.astype(jnp.bfloat16).reshape(1, blocks_dev, quarter, hidden)
        whole_rows = edge_exchange(rounded, quarters, False, 2)
        slot_sums = block_apply(
            backward_kernel, group_row, member, member_slot, weights_g, whole_rows,
            (slot_total, quarter, hidden),
        )
        arrived = lax.all_to_all(
            slot_sums, ("x", "c"), split_axis=0, concat_axis=0, tiled=True
        )
        dense = combine_apply(wanted_flat, arrived, blocks_dev)
        owned = lax.psum_scatter(dense, "z", scatter_dimension=0, tiled=True)
        adjoint = 0.9 * owned.reshape(row_count, hidden)
        factor = 0.1 if step_index + 1 < STEPS else 1.0
        gradient = gradient + factor * adjoint
    return (current, gradient)


def solution(mesh):
    devices = mesh.devices.reshape(Z_SIZE, X_SIZE, CORE_SIZE, mesh.shape["edge"])
    fine = Mesh(devices, ("z", "x", "c", "edge"))
    node = ("z", "x", "c")
    placed = (
        P((*node, "edge"), None),
        P((*node, "edge"), None),
        P(),
        P(node, None),
        P(node, None),
        P(node, None, "edge", None),
    )
    return jax.shard_map(
        per_device,
        mesh=fine,
        in_specs=placed,
        out_specs=(P((*node, "edge"), None), P((*node, "edge"), None)),
        check_vma=False,
    )
```

```python
import functools

import jax
import jax.numpy as jnp
from jax import lax
from jax.experimental import pallas as pl
from jax.experimental.pallas import tpu as pltpu
from jax.sharding import Mesh
from jax.sharding import PartitionSpec as P

MESH = pl.DeviceIdType.MESH

CAP = 2
STEPS = 2
Z_SIZE = 8
X_SIZE = 4
CORE_SIZE = 2
GROUP = 4
GROUPS_PER_STEP = 8
BLOCKS = 192


def forward_kernel(rows_ref, members_ref, slots_ref, v_ref, x_ref, out_ref):
    block_count = BLOCKS
    step = pl.program_id(0)
    quarters, _, quarter, hidden = out_ref.shape

    @pl.when(step == 0)
    def _():
        out_ref[...] = jnp.zeros_like(out_ref)

    def body(i, carry):
        g = step * GROUPS_PER_STEP + i

        j = rows_ref[g]
        pieces = []
        for m in range(GROUP):
            valid = members_ref[g * GROUP + m] < block_count
            piece = x_ref[slots_ref[g * GROUP + m]]
            pieces.append(jnp.where(valid, piece, jnp.zeros_like(piece)))
        sources = jnp.concatenate(pieces, axis=0)
        weights = v_ref[i]
        product = lax.dot_general(
            weights, sources, (((0,), (0,)), ((), ())), preferred_element_type=jnp.float32
        )
        out_ref[:, j] += product.reshape(quarters, quarter, hidden)
        return carry

    lax.fori_loop(0, GROUPS_PER_STEP, body, 0, unroll=4)


def backward_kernel(rows_ref, members_ref, slots_ref, v_ref, a_ref, out_ref):
    block_count = BLOCKS
    step = pl.program_id(0)
    quarters, _, quarter, hidden = a_ref.shape

    @pl.when(step == 0)
    def _():
        out_ref[...] = jnp.zeros_like(out_ref)

    def body(i, carry):
        g = step * GROUPS_PER_STEP + i

        j = rows_ref[g]
        sources = a_ref[:, j].reshape(quarters * quarter, hidden)
        weights = v_ref[i]
        product = jnp.dot(weights, sources, preferred_element_type=jnp.float32)
        for m in range(GROUP):
            s = slots_ref[g * GROUP + m]
            piece = product[m * quarter:(m + 1) * quarter]
            valid = members_ref[g * GROUP + m] < block_count
            out_ref[s] += jnp.where(valid, piece, jnp.zeros_like(piece))

        return carry

    lax.fori_loop(0, GROUPS_PER_STEP, body, 0, unroll=4)


def combine_kernel(want_ref, arrived_ref, out_ref):
    out_ref[...] = jnp.zeros_like(out_ref)
    lines = out_ref.shape[0]

    def body(q, carry):
        j = want_ref[q]
        piece = arrived_ref[q]
        out_ref[q // CAP % lines, jnp.maximum(j, 0)] += jnp.where(j >= 0, piece, jnp.zeros_like(piece))

        return carry

    lax.fori_loop(0, arrived_ref.shape[0], body, 0, unroll=8)


def edge_exchange_kernel(reduce, x_ref, out_ref, held, send_sem, recv_sem):
    count = held.shape[0]
    me = lax.axis_index("edge")
    barrier = pltpu.get_barrier_semaphore()
    for d in range(1, count):
        pl.semaphore_signal(
            barrier, inc=1, device_id={"edge": lax.rem(me + d, count)}, device_id_type=MESH
        )
    pl.semaphore_wait(barrier, count - 1)
    copies = []
    for d in range(1, count):
        peer = lax.rem(me + d, count)
        copy = pltpu.make_async_remote_copy(
            src_ref=x_ref.at[peer] if reduce else x_ref.at[0],
            dst_ref=held.at[me],
            send_sem=send_sem.at[d],
            recv_sem=recv_sem.at[d],
            device_id={"edge": peer},
            device_id_type=MESH,
        )
        copy.start()
        copies.append(copy)
    held[me] = x_ref[me] if reduce else x_ref[0]
    for copy in copies:
        copy.wait()
    if reduce:
        total = held[0]
        for q in range(1, count):
            total = total + held[q]
        out_ref[...] = total
    else:
        out_ref[...] = held[...]


def edge_exchange(chunks, count, reduce, collective_id):
    piece = chunks.shape[1:]
    out_shape = piece if reduce else (count,) + piece
    return pl.pallas_call(
        functools.partial(edge_exchange_kernel, reduce),
        out_shape=jax.ShapeDtypeStruct(out_shape, chunks.dtype),
        in_specs=[pl.BlockSpec(memory_space=pltpu.VMEM)],
        out_specs=pl.BlockSpec(memory_space=pltpu.VMEM),
        scratch_shapes=[
            pltpu.VMEM((count,) + piece, chunks.dtype),
            pltpu.SemaphoreType.DMA((count,)),
            pltpu.SemaphoreType.DMA((count,)),
        ],
        compiler_params=pltpu.CompilerParams(collective_id=collective_id, has_side_effects=True),
    )(chunks)


def block_apply(kernel, rows, members, slots, weights_g, dense, out_shape):
    group_count, depth, width = weights_g.shape
    return pl.pallas_call(
        kernel,
        out_shape=jax.ShapeDtypeStruct(out_shape, jnp.float32),
        grid_spec=pltpu.PrefetchScalarGridSpec(
            num_scalar_prefetch=3,
            grid=(group_count // GROUPS_PER_STEP,),
            in_specs=[
                pl.BlockSpec((GROUPS_PER_STEP, depth, width), lambda i, *_: (i, 0, 0)),
                pl.BlockSpec(dense.shape, lambda i, *_: (0,) * dense.ndim),
            ],
            out_specs=pl.BlockSpec(out_shape, lambda i, *_: (0,) * len(out_shape)),
        ),
        compiler_params=pltpu.CompilerParams(dimension_semantics=("arbitrary",)),
    )(rows, members, slots, weights_g, dense)


def combine_apply(wanted, arrived, blocks_dev):
    slot_total, quarter, hidden = arrived.shape
    lines = slot_total // (CAP * X_SIZE * CORE_SIZE)
    return pl.pallas_call(
        combine_kernel,
        out_shape=jax.ShapeDtypeStruct((lines, blocks_dev, quarter, hidden), jnp.float32),
        grid_spec=pltpu.PrefetchScalarGridSpec(
            num_scalar_prefetch=1,
            grid=(1,),
            in_specs=[pl.BlockSpec(arrived.shape, lambda i, w: (0, 0, 0))],
            out_specs=pl.BlockSpec(
                (lines, blocks_dev, quarter, hidden), lambda i, w: (0, 0, 0, 0)
            ),
        ),
    )(wanted, arrived)


def grouping(row_ids, blocks_dev):
    block_count = row_ids.shape[0]
    group_count = block_count // GROUP + blocks_dev
    hot = (row_ids[:, None] == jnp.arange(blocks_dev, dtype=jnp.int32)[None, :]).astype(jnp.float32)
    block_range = jnp.arange(block_count, dtype=jnp.int32)
    before = (block_range[None, :] < block_range[:, None]).astype(jnp.float32)
    rank = jnp.sum(
        jnp.dot(before, hot, precision=lax.Precision.HIGHEST) * hot, axis=1
    ).astype(jnp.int32)
    counts = jnp.sum(hot, axis=0).astype(jnp.int32)
    groups_per_row = (counts + GROUP - 1) // GROUP
    group_end = jnp.cumsum(groups_per_row)
    group_start = group_end - groups_per_row
    position = jnp.sum(hot * group_start[None, :].astype(jnp.float32), axis=1).astype(jnp.int32) * GROUP + rank
    member = jnp.full((group_count * GROUP,), block_count, jnp.int32).at[position].set(block_range)
    group_range = jnp.arange(group_count, dtype=jnp.int32)
    group_row = jnp.minimum(
        jnp.sum((group_range[:, None] >= group_end[None, :]).astype(jnp.int32), axis=1), blocks_dev - 1
    ).astype(jnp.int32)
    return member, group_row


def per_device(teleport, cotangent, fetch_table, block_row, block_slot, values):
    row_count, hidden = teleport.shape
    quarter = values.shape[2]
    blocks_dev = row_count // quarter
    slot_total = fetch_table.shape[1]
    quarters = lax.axis_size("edge")
    row_peers = X_SIZE * CORE_SIZE
    z_me = lax.axis_index("z")
    x_me = lax.axis_index("x")
    c_me = lax.axis_index("c")
    weights = values[0]
    row_ids = block_row[0]
    slot_ids = block_slot[0]

    owner = slot_ids // CAP
    placed_slots = (
        ((owner // CORE_SIZE % X_SIZE * CORE_SIZE + owner % CORE_SIZE) * Z_SIZE + owner // (CORE_SIZE * X_SIZE))
        * CAP
        + slot_ids % CAP
    ).astype(jnp.int32)

    peer_range = jnp.arange(row_peers, dtype=jnp.int32)
    z_range = jnp.arange(Z_SIZE, dtype=jnp.int32)
    peer_groups = (z_me * X_SIZE + peer_range // CORE_SIZE) * CORE_SIZE + peer_range % CORE_SIZE
    line_owners = (z_range * X_SIZE + x_me) * CORE_SIZE + c_me
    table_cols = line_owners[:, None] * CAP + jnp.arange(CAP, dtype=jnp.int32)[None, :]
    wanted = fetch_table[peer_groups[:, None, None], table_cols[None, :, :]]
    send_index = (z_range[None, :, None] * blocks_dev + jnp.maximum(wanted, 0)).reshape(-1)

    member, group_row = grouping(row_ids, blocks_dev)
    member_slot = jnp.take(placed_slots, member, axis=0, mode="clip")
    weights_g = jnp.take(weights, member, axis=0, mode="clip").reshape(
        member.shape[0] // GROUP, GROUP * quarter, weights.shape[2]
    )
    wanted_flat = wanted.reshape(-1)

    current = teleport
    for step_index in range(STEPS):
        rounded = current.astype(jnp.bfloat16).reshape(blocks_dev, quarter, hidden)
        line_blocks = lax.all_gather(rounded, "z", axis=0, tiled=True)
        outgoing = jnp.take(line_blocks, send_index, axis=0)
        received = lax.all_to_all(
            outgoing, ("x", "c"), split_axis=0, concat_axis=0, tiled=True
        )
        partial = block_apply(
            forward_kernel, group_row, member, member_slot, weights_g, received,
            (quarters, blocks_dev, quarter, hidden),
        )
        summed = edge_exchange(partial, quarters, True, 1)
        current = 0.9 * summed.reshape(row_count, hidden) + 0.1 * teleport

    adjoint = cotangent
    gradient = 0.1 * cotangent
    for step_index in range(STEPS):
        rounded = adjoint.astype(jnp.bfloat16).reshape(1, blocks_dev, quarter, hidden)
        whole_rows = edge_exchange(rounded, quarters, False, 2)
        slot_sums = block_apply(
            backward_kernel, group_row, member, member_slot, weights_g, whole_rows,
            (slot_total, quarter, hidden),
        )
        arrived = lax.all_to_all(
            slot_sums, ("x", "c"), split_axis=0, concat_axis=0, tiled=True
        )
        dense = combine_apply(wanted_flat, arrived, blocks_dev)
        owned = lax.psum_scatter(dense, "z", scatter_dimension=0, tiled=True)
        adjoint = 0.9 * owned.reshape(row_count, hidden)
        factor = 0.1 if step_index + 1 < STEPS else 1.0
        gradient = gradient + factor * adjoint
    return (current, gradient)


def solution(mesh):
    devices = mesh.devices.reshape(Z_SIZE, X_SIZE, CORE_SIZE, mesh.shape["edge"])
    fine = Mesh(devices, ("z", "x", "c", "edge"))
    node = ("z", "x", "c")
    placed = (
        P((*node, "edge"), None),
        P((*node, "edge"), None),
        P(),
        P(node, None),
        P(node, None),
        P(node, None, "edge", None),
    )
    return jax.shard_map(
        per_device,
        mesh=fine,
        in_specs=placed,
        out_specs=(P((*node, "edge"), None), P((*node, "edge"), None)),
        check_vma=False,
    )
```

```python
import functools

import jax
import jax.numpy as jnp
from jax import lax
from jax.experimental import pallas as pl
from jax.experimental.pallas import tpu as pltpu
from jax.sharding import Mesh
from jax.sharding import PartitionSpec as P

MESH = pl.DeviceIdType.MESH

CAP = 2
STEPS = 2
Z_SIZE = 8
X_SIZE = 4
CORE_SIZE = 2
GROUP = 4
GROUPS_PER_STEP = 14
BLOCKS = 192


def forward_kernel(rows_ref, members_ref, slots_ref, v_ref, x_ref, out_ref):
    block_count = BLOCKS
    step = pl.program_id(0)
    quarters, _, quarter, hidden = out_ref.shape

    @pl.when(step == 0)
    def _():
        out_ref[...] = jnp.zeros_like(out_ref)

    def body(i, carry):
        g = step * GROUPS_PER_STEP + i

        j = rows_ref[g]
        pieces = []
        for m in range(GROUP):
            valid = members_ref[g * GROUP + m] < block_count
            piece = x_ref[slots_ref[g * GROUP + m]]
            pieces.append(jnp.where(valid, piece, jnp.zeros_like(piece)))
        sources = jnp.concatenate(pieces, axis=0)
        weights = v_ref[i]
        product = lax.dot_general(
            weights, sources, (((0,), (0,)), ((), ())), preferred_element_type=jnp.float32
        )
        out_ref[:, j] += product.reshape(quarters, quarter, hidden)
        return carry

    lax.fori_loop(0, GROUPS_PER_STEP, body, 0, unroll=7)


def backward_kernel(rows_ref, members_ref, slots_ref, v_ref, a_ref, out_ref):
    block_count = BLOCKS
    step = pl.program_id(0)
    quarters, _, quarter, hidden = a_ref.shape

    @pl.when(step == 0)
    def _():
        out_ref[...] = jnp.zeros_like(out_ref)

    def body(i, carry):
        g = step * GROUPS_PER_STEP + i

        j = rows_ref[g]
        sources = a_ref[:, j].reshape(quarters * quarter, hidden)
        weights = v_ref[i]
        product = jnp.dot(weights, sources, preferred_element_type=jnp.float32)
        for m in range(GROUP):
            s = slots_ref[g * GROUP + m]
            piece = product[m * quarter:(m + 1) * quarter]
            valid = members_ref[g * GROUP + m] < block_count
            out_ref[s] += jnp.where(valid, piece, jnp.zeros_like(piece))

        return carry

    lax.fori_loop(0, GROUPS_PER_STEP, body, 0, unroll=7)


def combine_kernel(want_ref, arrived_ref, out_ref):
    out_ref[...] = jnp.zeros_like(out_ref)
    lines = out_ref.shape[0]

    def body(q, carry):
        j = want_ref[q]
        piece = arrived_ref[q]
        out_ref[q // CAP % lines, jnp.maximum(j, 0)] += jnp.where(j >= 0, piece, jnp.zeros_like(piece))

        return carry

    lax.fori_loop(0, arrived_ref.shape[0], body, 0, unroll=8)


def edge_exchange_kernel(reduce, x_ref, out_ref, held, send_sem, recv_sem):
    count = held.shape[0]
    me = lax.axis_index("edge")
    barrier = pltpu.get_barrier_semaphore()
    for d in range(1, count):
        pl.semaphore_signal(
            barrier, inc=1, device_id={"edge": lax.rem(me + d, count)}, device_id_type=MESH
        )
    pl.semaphore_wait(barrier, count - 1)
    copies = []
    for d in range(1, count):
        peer = lax.rem(me + d, count)
        copy = pltpu.make_async_remote_copy(
            src_ref=x_ref.at[peer] if reduce else x_ref.at[0],
            dst_ref=held.at[me],
            send_sem=send_sem.at[d],
            recv_sem=recv_sem.at[d],
            device_id={"edge": peer},
            device_id_type=MESH,
        )
        copy.start()
        copies.append(copy)
    held[me] = x_ref[me] if reduce else x_ref[0]
    for copy in copies:
        copy.wait()
    if reduce:
        total = held[0]
        for q in range(1, count):
            total = total + held[q]
        out_ref[...] = total
    else:
        out_ref[...] = held[...]


def edge_exchange(chunks, count, reduce, collective_id):
    piece = chunks.shape[1:]
    out_shape = piece if reduce else (count,) + piece
    return pl.pallas_call(
        functools.partial(edge_exchange_kernel, reduce),
        out_shape=jax.ShapeDtypeStruct(out_shape, chunks.dtype),
        in_specs=[pl.BlockSpec(memory_space=pltpu.VMEM)],
        out_specs=pl.BlockSpec(memory_space=pltpu.VMEM),
        scratch_shapes=[
            pltpu.VMEM((count,) + piece, chunks.dtype),
            pltpu.SemaphoreType.DMA((count,)),
            pltpu.SemaphoreType.DMA((count,)),
        ],
        compiler_params=pltpu.CompilerParams(collective_id=collective_id, has_side_effects=True),
    )(chunks)


def block_apply(kernel, rows, members, slots, weights_g, dense, out_shape):
    group_count, depth, width = weights_g.shape
    return pl.pallas_call(
        kernel,
        out_shape=jax.ShapeDtypeStruct(out_shape, jnp.float32),
        grid_spec=pltpu.PrefetchScalarGridSpec(
            num_scalar_prefetch=3,
            grid=(group_count // GROUPS_PER_STEP,),
            in_specs=[
                pl.BlockSpec((GROUPS_PER_STEP, depth, width), lambda i, *_: (i, 0, 0)),
                pl.BlockSpec(dense.shape, lambda i, *_: (0,) * dense.ndim),
            ],
            out_specs=pl.BlockSpec(out_shape, lambda i, *_: (0,) * len(out_shape)),
        ),
        compiler_params=pltpu.CompilerParams(dimension_semantics=("arbitrary",)),
    )(rows, members, slots, weights_g, dense)


def combine_apply(wanted, arrived, blocks_dev):
    slot_total, quarter, hidden = arrived.shape
    lines = slot_total // (CAP * X_SIZE * CORE_SIZE)
    return pl.pallas_call(
        combine_kernel,
        out_shape=jax.ShapeDtypeStruct((lines, blocks_dev, quarter, hidden), jnp.float32),
        grid_spec=pltpu.PrefetchScalarGridSpec(
            num_scalar_prefetch=1,
            grid=(1,),
            in_specs=[pl.BlockSpec(arrived.shape, lambda i, w: (0, 0, 0))],
            out_specs=pl.BlockSpec(
                (lines, blocks_dev, quarter, hidden), lambda i, w: (0, 0, 0, 0)
            ),
        ),
    )(wanted, arrived)


def grouping(row_ids, blocks_dev):
    block_count = row_ids.shape[0]
    group_count = block_count // GROUP + blocks_dev
    hot = (row_ids[:, None] == jnp.arange(blocks_dev, dtype=jnp.int32)[None, :]).astype(jnp.float32)
    block_range = jnp.arange(block_count, dtype=jnp.int32)
    before = (block_range[None, :] < block_range[:, None]).astype(jnp.float32)
    rank = jnp.sum(
        jnp.dot(before, hot, precision=lax.Precision.HIGHEST) * hot, axis=1
    ).astype(jnp.int32)
    counts = jnp.sum(hot, axis=0).astype(jnp.int32)
    groups_per_row = (counts + GROUP - 1) // GROUP
    group_end = jnp.cumsum(groups_per_row)
    group_start = group_end - groups_per_row
    position = jnp.sum(hot * group_start[None, :].astype(jnp.float32), axis=1).astype(jnp.int32) * GROUP + rank
    member = jnp.full((group_count * GROUP,), block_count, jnp.int32).at[position].set(block_range)
    group_range = jnp.arange(group_count, dtype=jnp.int32)
    group_row = jnp.minimum(
        jnp.sum((group_range[:, None] >= group_end[None, :]).astype(jnp.int32), axis=1), blocks_dev - 1
    ).astype(jnp.int32)
    return member, group_row


def per_device(teleport, cotangent, fetch_table, block_row, block_slot, values):
    row_count, hidden = teleport.shape
    quarter = values.shape[2]
    blocks_dev = row_count // quarter
    slot_total = fetch_table.shape[1]
    quarters = lax.axis_size("edge")
    row_peers = X_SIZE * CORE_SIZE
    z_me = lax.axis_index("z")
    x_me = lax.axis_index("x")
    c_me = lax.axis_index("c")
    weights = values[0]
    row_ids = block_row[0]
    slot_ids = block_slot[0]

    owner = slot_ids // CAP
    placed_slots = (
        ((owner // CORE_SIZE % X_SIZE * CORE_SIZE + owner % CORE_SIZE) * Z_SIZE + owner // (CORE_SIZE * X_SIZE))
        * CAP
        + slot_ids % CAP
    ).astype(jnp.int32)

    peer_range = jnp.arange(row_peers, dtype=jnp.int32)
    z_range = jnp.arange(Z_SIZE, dtype=jnp.int32)
    peer_groups = (z_me * X_SIZE + peer_range // CORE_SIZE) * CORE_SIZE + peer_range % CORE_SIZE
    line_owners = (z_range * X_SIZE + x_me) * CORE_SIZE + c_me
    table_cols = line_owners[:, None] * CAP + jnp.arange(CAP, dtype=jnp.int32)[None, :]
    wanted = fetch_table[peer_groups[:, None, None], table_cols[None, :, :]]
    send_index = (z_range[None, :, None] * blocks_dev + jnp.maximum(wanted, 0)).reshape(-1)

    member, group_row = grouping(row_ids, blocks_dev)
    member_slot = jnp.take(placed_slots, member, axis=0, mode="clip")
    weights_g = jnp.take(weights, member, axis=0, mode="clip").reshape(
        member.shape[0] // GROUP, GROUP * quarter, weights.shape[2]
    )
    wanted_flat = wanted.reshape(-1)

    current = teleport
    for step_index in range(STEPS):
        rounded = current.astype(jnp.bfloat16).reshape(blocks_dev, quarter, hidden)
        line_blocks = lax.all_gather(rounded, "z", axis=0, tiled=True)
        outgoing = jnp.take(line_blocks, send_index, axis=0)
        received = lax.all_to_all(
            outgoing, ("x", "c"), split_axis=0, concat_axis=0, tiled=True
        )
        partial = block_apply(
            forward_kernel, group_row, member, member_slot, weights_g, received,
            (quarters, blocks_dev, quarter, hidden),
        )
        summed = edge_exchange(partial, quarters, True, 1)
        current = 0.9 * summed.reshape(row_count, hidden) + 0.1 * teleport

    adjoint = cotangent
    gradient = 0.1 * cotangent
    for step_index in range(STEPS):
        rounded = adjoint.astype(jnp.bfloat16).reshape(1, blocks_dev, quarter, hidden)
        whole_rows = edge_exchange(rounded, quarters, False, 2)
        slot_sums = block_apply(
            backward_kernel, group_row, member, member_slot, weights_g, whole_rows,
            (slot_total, quarter, hidden),
        )
        arrived = lax.all_to_all(
            slot_sums, ("x", "c"), split_axis=0, concat_axis=0, tiled=True
        )
        dense = combine_apply(wanted_flat, arrived, blocks_dev)
        owned = lax.psum_scatter(dense, "z", scatter_dimension=0, tiled=True)
        adjoint = 0.9 * owned.reshape(row_count, hidden)
        factor = 0.1 if step_index + 1 < STEPS else 1.0
        gradient = gradient + factor * adjoint
    return (current, gradient)


def solution(mesh):
    devices = mesh.devices.reshape(Z_SIZE, X_SIZE, CORE_SIZE, mesh.shape["edge"])
    fine = Mesh(devices, ("z", "x", "c", "edge"))
    node = ("z", "x", "c")
    placed = (
        P((*node, "edge"), None),
        P((*node, "edge"), None),
        P(),
        P(node, None),
        P(node, None),
        P(node, None, "edge", None),
    )
    return jax.shard_map(
        per_device,
        mesh=fine,
        in_specs=placed,
        out_specs=(P((*node, "edge"), None), P((*node, "edge"), None)),
        check_vma=False,
    )
```

```python
import functools

import jax
import jax.numpy as jnp
from jax import lax
from jax.experimental import pallas as pl
from jax.experimental.pallas import tpu as pltpu
from jax.sharding import Mesh
from jax.sharding import PartitionSpec as P

MESH = pl.DeviceIdType.MESH

CAP = 2
STEPS = 2
Z_SIZE = 8
X_SIZE = 4
CORE_SIZE = 2
GROUP = 4
GROUPS_PER_STEP = 28
BLOCKS = 192


def forward_kernel(rows_ref, members_ref, slots_ref, v_ref, x_ref, out_ref):
    block_count = BLOCKS
    step = pl.program_id(0)
    quarters, _, quarter, hidden = out_ref.shape

    @pl.when(step == 0)
    def _():
        out_ref[...] = jnp.zeros_like(out_ref)

    def body(i, carry):
        g = step * GROUPS_PER_STEP + i

        j = rows_ref[g]
        pieces = []
        for m in range(GROUP):
            valid = members_ref[g * GROUP + m] < block_count
            piece = x_ref[slots_ref[g * GROUP + m]]
            pieces.append(jnp.where(valid, piece, jnp.zeros_like(piece)))
        sources = jnp.concatenate(pieces, axis=0)
        weights = v_ref[i]
        product = lax.dot_general(
            weights, sources, (((0,), (0,)), ((), ())), preferred_element_type=jnp.float32
        )
        out_ref[:, j] += product.reshape(quarters, quarter, hidden)
        return carry

    lax.fori_loop(0, GROUPS_PER_STEP, body, 0, unroll=7)


def backward_kernel(rows_ref, members_ref, slots_ref, v_ref, a_ref, out_ref):
    block_count = BLOCKS
    step = pl.program_id(0)
    quarters, _, quarter, hidden = a_ref.shape

    @pl.when(step == 0)
    def _():
        out_ref[...] = jnp.zeros_like(out_ref)

    def body(i, carry):
        g = step * GROUPS_PER_STEP + i

        j = rows_ref[g]
        sources = a_ref[:, j].reshape(quarters * quarter, hidden)
        weights = v_ref[i]
        product = jnp.dot(weights, sources, preferred_element_type=jnp.float32)
        for m in range(GROUP):
            s = slots_ref[g * GROUP + m]
            piece = product[m * quarter:(m + 1) * quarter]
            valid = members_ref[g * GROUP + m] < block_count
            out_ref[s] += jnp.where(valid, piece, jnp.zeros_like(piece))

        return carry

    lax.fori_loop(0, GROUPS_PER_STEP, body, 0, unroll=7)


def combine_kernel(want_ref, arrived_ref, out_ref):
    out_ref[...] = jnp.zeros_like(out_ref)
    lines = out_ref.shape[0]

    def body(q, carry):
        j = want_ref[q]
        piece = arrived_ref[q]
        out_ref[q // CAP % lines, jnp.maximum(j, 0)] += jnp.where(j >= 0, piece, jnp.zeros_like(piece))

        return carry

    lax.fori_loop(0, arrived_ref.shape[0], body, 0, unroll=8)


def edge_exchange_kernel(reduce, x_ref, out_ref, held, send_sem, recv_sem):
    count = held.shape[0]
    me = lax.axis_index("edge")
    barrier = pltpu.get_barrier_semaphore()
    for d in range(1, count):
        pl.semaphore_signal(
            barrier, inc=1, device_id={"edge": lax.rem(me + d, count)}, device_id_type=MESH
        )
    pl.semaphore_wait(barrier, count - 1)
    copies = []
    for d in range(1, count):
        peer = lax.rem(me + d, count)
        copy = pltpu.make_async_remote_copy(
            src_ref=x_ref.at[peer] if reduce else x_ref.at[0],
            dst_ref=held.at[me],
            send_sem=send_sem.at[d],
            recv_sem=recv_sem.at[d],
            device_id={"edge": peer},
            device_id_type=MESH,
        )
        copy.start()
        copies.append(copy)
    held[me] = x_ref[me] if reduce else x_ref[0]
    for copy in copies:
        copy.wait()
    if reduce:
        total = held[0]
        for q in range(1, count):
            total = total + held[q]
        out_ref[...] = total
    else:
        out_ref[...] = held[...]


def edge_exchange(chunks, count, reduce, collective_id):
    piece = chunks.shape[1:]
    out_shape = piece if reduce else (count,) + piece
    return pl.pallas_call(
        functools.partial(edge_exchange_kernel, reduce),
        out_shape=jax.ShapeDtypeStruct(out_shape, chunks.dtype),
        in_specs=[pl.BlockSpec(memory_space=pltpu.VMEM)],
        out_specs=pl.BlockSpec(memory_space=pltpu.VMEM),
        scratch_shapes=[
            pltpu.VMEM((count,) + piece, chunks.dtype),
            pltpu.SemaphoreType.DMA((count,)),
            pltpu.SemaphoreType.DMA((count,)),
        ],
        compiler_params=pltpu.CompilerParams(collective_id=collective_id, has_side_effects=True),
    )(chunks)


def block_apply(kernel, rows, members, slots, weights_g, dense, out_shape):
    group_count, depth, width = weights_g.shape
    return pl.pallas_call(
        kernel,
        out_shape=jax.ShapeDtypeStruct(out_shape, jnp.float32),
        grid_spec=pltpu.PrefetchScalarGridSpec(
            num_scalar_prefetch=3,
            grid=(group_count // GROUPS_PER_STEP,),
            in_specs=[
                pl.BlockSpec((GROUPS_PER_STEP, depth, width), lambda i, *_: (i, 0, 0)),
                pl.BlockSpec(dense.shape, lambda i, *_: (0,) * dense.ndim),
            ],
            out_specs=pl.BlockSpec(out_shape, lambda i, *_: (0,) * len(out_shape)),
        ),
        compiler_params=pltpu.CompilerParams(dimension_semantics=("arbitrary",)),
    )(rows, members, slots, weights_g, dense)


def combine_apply(wanted, arrived, blocks_dev):
    slot_total, quarter, hidden = arrived.shape
    lines = slot_total // (CAP * X_SIZE * CORE_SIZE)
    return pl.pallas_call(
        combine_kernel,
        out_shape=jax.ShapeDtypeStruct((lines, blocks_dev, quarter, hidden), jnp.float32),
        grid_spec=pltpu.PrefetchScalarGridSpec(
            num_scalar_prefetch=1,
            grid=(1,),
            in_specs=[pl.BlockSpec(arrived.shape, lambda i, w: (0, 0, 0))],
            out_specs=pl.BlockSpec(
                (lines, blocks_dev, quarter, hidden), lambda i, w: (0, 0, 0, 0)
            ),
        ),
    )(wanted, arrived)


def grouping(row_ids, blocks_dev):
    block_count = row_ids.shape[0]
    group_count = block_count // GROUP + blocks_dev
    hot = (row_ids[:, None] == jnp.arange(blocks_dev, dtype=jnp.int32)[None, :]).astype(jnp.float32)
    block_range = jnp.arange(block_count, dtype=jnp.int32)
    before = (block_range[None, :] < block_range[:, None]).astype(jnp.float32)
    rank = jnp.sum(
        jnp.dot(before, hot, precision=lax.Precision.HIGHEST) * hot, axis=1
    ).astype(jnp.int32)
    counts = jnp.sum(hot, axis=0).astype(jnp.int32)
    groups_per_row = (counts + GROUP - 1) // GROUP
    group_end = jnp.cumsum(groups_per_row)
    group_start = group_end - groups_per_row
    position = jnp.sum(hot * group_start[None, :].astype(jnp.float32), axis=1).astype(jnp.int32) * GROUP + rank
    member = jnp.full((group_count * GROUP,), block_count, jnp.int32).at[position].set(block_range)
    group_range = jnp.arange(group_count, dtype=jnp.int32)
    group_row = jnp.minimum(
        jnp.sum((group_range[:, None] >= group_end[None, :]).astype(jnp.int32), axis=1), blocks_dev - 1
    ).astype(jnp.int32)
    return member, group_row


def per_device(teleport, cotangent, fetch_table, block_row, block_slot, values):
    row_count, hidden = teleport.shape
    quarter = values.shape[2]
    blocks_dev = row_count // quarter
    slot_total = fetch_table.shape[1]
    quarters = lax.axis_size("edge")
    row_peers = X_SIZE * CORE_SIZE
    z_me = lax.axis_index("z")
    x_me = lax.axis_index("x")
    c_me = lax.axis_index("c")
    weights = values[0]
    row_ids = block_row[0]
    slot_ids = block_slot[0]

    owner = slot_ids // CAP
    placed_slots = (
        ((owner // CORE_SIZE % X_SIZE * CORE_SIZE + owner % CORE_SIZE) * Z_SIZE + owner // (CORE_SIZE * X_SIZE))
        * CAP
        + slot_ids % CAP
    ).astype(jnp.int32)

    peer_range = jnp.arange(row_peers, dtype=jnp.int32)
    z_range = jnp.arange(Z_SIZE, dtype=jnp.int32)
    peer_groups = (z_me * X_SIZE + peer_range // CORE_SIZE) * CORE_SIZE + peer_range % CORE_SIZE
    line_owners = (z_range * X_SIZE + x_me) * CORE_SIZE + c_me
    table_cols = line_owners[:, None] * CAP + jnp.arange(CAP, dtype=jnp.int32)[None, :]
    wanted = fetch_table[peer_groups[:, None, None], table_cols[None, :, :]]
    send_index = (z_range[None, :, None] * blocks_dev + jnp.maximum(wanted, 0)).reshape(-1)

    member, group_row = grouping(row_ids, blocks_dev)
    member_slot = jnp.take(placed_slots, member, axis=0, mode="clip")
    weights_g = jnp.take(weights, member, axis=0, mode="clip").reshape(
        member.shape[0] // GROUP, GROUP * quarter, weights.shape[2]
    )
    wanted_flat = wanted.reshape(-1)

    current = teleport
    for step_index in range(STEPS):
        rounded = current.astype(jnp.bfloat16).reshape(blocks_dev, quarter, hidden)
        line_blocks = lax.all_gather(rounded, "z", axis=0, tiled=True)
        outgoing = jnp.take(line_blocks, send_index, axis=0)
        received = lax.all_to_all(
            outgoing, ("x", "c"), split_axis=0, concat_axis=0, tiled=True
        )
        partial = block_apply(
            forward_kernel, group_row, member, member_slot, weights_g, received,
            (quarters, blocks_dev, quarter, hidden),
        )
        summed = edge_exchange(partial, quarters, True, 1)
        current = 0.9 * summed.reshape(row_count, hidden) + 0.1 * teleport

    adjoint = cotangent
    gradient = 0.1 * cotangent
    for step_index in range(STEPS):
        rounded = adjoint.astype(jnp.bfloat16).reshape(1, blocks_dev, quarter, hidden)
        whole_rows = edge_exchange(rounded, quarters, False, 2)
        slot_sums = block_apply(
            backward_kernel, group_row, member, member_slot, weights_g, whole_rows,
            (slot_total, quarter, hidden),
        )
        arrived = lax.all_to_all(
            slot_sums, ("x", "c"), split_axis=0, concat_axis=0, tiled=True
        )
        dense = combine_apply(wanted_flat, arrived, blocks_dev)
        owned = lax.psum_scatter(dense, "z", scatter_dimension=0, tiled=True)
        adjoint = 0.9 * owned.reshape(row_count, hidden)
        factor = 0.1 if step_index + 1 < STEPS else 1.0
        gradient = gradient + factor * adjoint
    return (current, gradient)


def solution(mesh):
    devices = mesh.devices.reshape(Z_SIZE, X_SIZE, CORE_SIZE, mesh.shape["edge"])
    fine = Mesh(devices, ("z", "x", "c", "edge"))
    node = ("z", "x", "c")
    placed = (
        P((*node, "edge"), None),
        P((*node, "edge"), None),
        P(),
        P(node, None),
        P(node, None),
        P(node, None, "edge", None),
    )
    return jax.shard_map(
        per_device,
        mesh=fine,
        in_specs=placed,
        out_specs=(P((*node, "edge"), None), P((*node, "edge"), None)),
        check_vma=False,
    )
```

```python
import functools

import jax
import jax.numpy as jnp
from jax import lax
from jax.experimental import pallas as pl
from jax.experimental.pallas import tpu as pltpu
from jax.sharding import Mesh
from jax.sharding import PartitionSpec as P

MESH = pl.DeviceIdType.MESH

CAP = 2
STEPS = 2
Z_SIZE = 8
X_SIZE = 4
CORE_SIZE = 2
GROUP = 4
GROUPS_PER_STEP = 28
BLOCKS = 192


def forward_kernel(rows_ref, members_ref, slots_ref, v_ref, x_ref, out_ref):
    block_count = BLOCKS
    step = pl.program_id(0)
    quarters, _, quarter, hidden = out_ref.shape

    @pl.when(step == 0)
    def _():
        out_ref[...] = jnp.zeros_like(out_ref)

    def body(i, carry):
        g = step * GROUPS_PER_STEP + i

        j = rows_ref[g]
        pieces = []
        for m in range(GROUP):
            valid = members_ref[g * GROUP + m] < block_count
            piece = x_ref[slots_ref[g * GROUP + m]]
            pieces.append(jnp.where(valid, piece, jnp.zeros_like(piece)))
        sources = jnp.concatenate(pieces, axis=0)
        weights = v_ref[i]
        product = lax.dot_general(
            weights, sources, (((0,), (0,)), ((), ())), preferred_element_type=jnp.float32
        )
        out_ref[:, j] += product.reshape(quarters, quarter, hidden)
        return carry

    lax.fori_loop(0, GROUPS_PER_STEP, body, 0, unroll=7)


def backward_kernel(rows_ref, members_ref, slots_ref, v_ref, a_ref, out_ref):
    block_count = BLOCKS
    step = pl.program_id(0)
    quarters, _, quarter, hidden = a_ref.shape

    @pl.when(step == 0)
    def _():
        out_ref[...] = jnp.zeros_like(out_ref)

    def body(i, carry):
        g = step * GROUPS_PER_STEP + i

        j = rows_ref[g]
        sources = a_ref[:, j].reshape(quarters * quarter, hidden)
        weights = v_ref[i]
        product = jnp.dot(weights, sources, preferred_element_type=jnp.float32)
        for m in range(GROUP):
            s = slots_ref[g * GROUP + m]
            piece = product[m * quarter:(m + 1) * quarter]
            valid = members_ref[g * GROUP + m] < block_count
            out_ref[s] += jnp.where(valid, piece, jnp.zeros_like(piece))

        return carry

    lax.fori_loop(0, GROUPS_PER_STEP, body, 0, unroll=7)


def combine_kernel(want_ref, arrived_ref, out_ref):
    out_ref[...] = jnp.zeros_like(out_ref)
    lines = out_ref.shape[0]

    def body(q, carry):
        j = want_ref[q]
        piece = arrived_ref[q]
        out_ref[q // CAP % lines, jnp.maximum(j, 0)] += jnp.where(j >= 0, piece, jnp.zeros_like(piece))

        return carry

    lax.fori_loop(0, arrived_ref.shape[0], body, 0, unroll=8)


def edge_exchange_kernel(reduce, x_ref, base_ref, out_ref, held, send_sem, recv_sem):
    count = held.shape[0]
    me = lax.axis_index("edge")
    barrier = pltpu.get_barrier_semaphore()
    for d in range(1, count):
        pl.semaphore_signal(
            barrier, inc=1, device_id={"edge": lax.rem(me + d, count)}, device_id_type=MESH
        )
    pl.semaphore_wait(barrier, count - 1)
    copies = []
    for d in range(1, count):
        peer = lax.rem(me + d, count)
        copy = pltpu.make_async_remote_copy(
            src_ref=x_ref.at[peer] if reduce else x_ref.at[0],
            dst_ref=held.at[me],
            send_sem=send_sem.at[d],
            recv_sem=recv_sem.at[d],
            device_id={"edge": peer},
            device_id_type=MESH,
        )
        copy.start()
        copies.append(copy)
    held[me] = x_ref[me] if reduce else x_ref[0]
    for copy in copies:
        copy.wait()
    if reduce:
        total = held[0]
        for q in range(1, count):
            total = total + held[q]
        out_ref[...] = 0.9 * total + 0.1 * base_ref[...]
    else:
        out_ref[...] = held[...]


def edge_exchange(chunks, count, reduce, collective_id, base):
    piece = chunks.shape[1:]
    out_shape = piece if reduce else (count,) + piece
    return pl.pallas_call(
        functools.partial(edge_exchange_kernel, reduce),
        out_shape=jax.ShapeDtypeStruct(out_shape, chunks.dtype),
        in_specs=[pl.BlockSpec(memory_space=pltpu.VMEM)] * 2,
        out_specs=pl.BlockSpec(memory_space=pltpu.VMEM),
        scratch_shapes=[
            pltpu.VMEM((count,) + piece, chunks.dtype),
            pltpu.SemaphoreType.DMA((count,)),
            pltpu.SemaphoreType.DMA((count,)),
        ],
        compiler_params=pltpu.CompilerParams(collective_id=collective_id, has_side_effects=True),
    )(chunks, base)


def block_apply(kernel, rows, members, slots, weights_g, dense, out_shape):
    group_count, depth, width = weights_g.shape
    return pl.pallas_call(
        kernel,
        out_shape=jax.ShapeDtypeStruct(out_shape, jnp.float32),
        grid_spec=pltpu.PrefetchScalarGridSpec(
            num_scalar_prefetch=3,
            grid=(group_count // GROUPS_PER_STEP,),
            in_specs=[
                pl.BlockSpec((GROUPS_PER_STEP, depth, width), lambda i, *_: (i, 0, 0)),
                pl.BlockSpec(dense.shape, lambda i, *_: (0,) * dense.ndim),
            ],
            out_specs=pl.BlockSpec(out_shape, lambda i, *_: (0,) * len(out_shape)),
        ),
        compiler_params=pltpu.CompilerParams(dimension_semantics=("arbitrary",)),
    )(rows, members, slots, weights_g, dense)


def combine_apply(wanted, arrived, blocks_dev):
    slot_total, quarter, hidden = arrived.shape
    lines = slot_total // (CAP * X_SIZE * CORE_SIZE)
    return pl.pallas_call(
        combine_kernel,
        out_shape=jax.ShapeDtypeStruct((lines, blocks_dev, quarter, hidden), jnp.float32),
        grid_spec=pltpu.PrefetchScalarGridSpec(
            num_scalar_prefetch=1,
            grid=(1,),
            in_specs=[pl.BlockSpec(arrived.shape, lambda i, w: (0, 0, 0))],
            out_specs=pl.BlockSpec(
                (lines, blocks_dev, quarter, hidden), lambda i, w: (0, 0, 0, 0)
            ),
        ),
    )(wanted, arrived)


def grouping(row_ids, blocks_dev):
    block_count = row_ids.shape[0]
    group_count = block_count // GROUP + blocks_dev
    hot = (row_ids[:, None] == jnp.arange(blocks_dev, dtype=jnp.int32)[None, :]).astype(jnp.float32)
    block_range = jnp.arange(block_count, dtype=jnp.int32)
    before = (block_range[None, :] < block_range[:, None]).astype(jnp.float32)
    rank = jnp.sum(
        jnp.dot(before, hot, precision=lax.Precision.HIGHEST) * hot, axis=1
    ).astype(jnp.int32)
    counts = jnp.sum(hot, axis=0).astype(jnp.int32)
    groups_per_row = (counts + GROUP - 1) // GROUP
    group_end = jnp.cumsum(groups_per_row)
    group_start = group_end - groups_per_row
    position = jnp.sum(hot * group_start[None, :].astype(jnp.float32), axis=1).astype(jnp.int32) * GROUP + rank
    member = jnp.full((group_count * GROUP,), block_count, jnp.int32).at[position].set(block_range)
    group_range = jnp.arange(group_count, dtype=jnp.int32)
    group_row = jnp.minimum(
        jnp.sum((group_range[:, None] >= group_end[None, :]).astype(jnp.int32), axis=1), blocks_dev - 1
    ).astype(jnp.int32)
    return member, group_row


def per_device(teleport, cotangent, fetch_table, block_row, block_slot, values):
    row_count, hidden = teleport.shape
    quarter = values.shape[2]
    blocks_dev = row_count // quarter
    slot_total = fetch_table.shape[1]
    quarters = lax.axis_size("edge")
    row_peers = X_SIZE * CORE_SIZE
    z_me = lax.axis_index("z")
    x_me = lax.axis_index("x")
    c_me = lax.axis_index("c")
    weights = values[0]
    row_ids = block_row[0]
    slot_ids = block_slot[0]

    owner = slot_ids // CAP
    placed_slots = (
        ((owner // CORE_SIZE % X_SIZE * CORE_SIZE + owner % CORE_SIZE) * Z_SIZE + owner // (CORE_SIZE * X_SIZE))
        * CAP
        + slot_ids % CAP
    ).astype(jnp.int32)

    peer_range = jnp.arange(row_peers, dtype=jnp.int32)
    z_range = jnp.arange(Z_SIZE, dtype=jnp.int32)
    peer_groups = (z_me * X_SIZE + peer_range // CORE_SIZE) * CORE_SIZE + peer_range % CORE_SIZE
    line_owners = (z_range * X_SIZE + x_me) * CORE_SIZE + c_me
    table_cols = line_owners[:, None] * CAP + jnp.arange(CAP, dtype=jnp.int32)[None, :]
    wanted = fetch_table[peer_groups[:, None, None], table_cols[None, :, :]]
    send_index = (z_range[None, :, None] * blocks_dev + jnp.maximum(wanted, 0)).reshape(-1)

    member, group_row = grouping(row_ids, blocks_dev)
    member_slot = jnp.take(placed_slots, member, axis=0, mode="clip")
    weights_g = jnp.take(weights, member, axis=0, mode="clip").reshape(
        member.shape[0] // GROUP, GROUP * quarter, weights.shape[2]
    )
    wanted_flat = wanted.reshape(-1)

    current = teleport
    for step_index in range(STEPS):
        rounded = current.astype(jnp.bfloat16).reshape(blocks_dev, quarter, hidden)
        line_blocks = lax.all_gather(rounded, "z", axis=0, tiled=True)
        outgoing = jnp.take(line_blocks, send_index, axis=0)
        received = lax.all_to_all(
            outgoing, ("x", "c"), split_axis=0, concat_axis=0, tiled=True
        )
        partial = block_apply(
            forward_kernel, group_row, member, member_slot, weights_g, received,
            (quarters, blocks_dev, quarter, hidden),
        )
        current = edge_exchange(
            partial, quarters, True, 1, teleport.reshape(blocks_dev, quarter, hidden)
        ).reshape(row_count, hidden)

    adjoint = cotangent
    gradient = 0.1 * cotangent
    for step_index in range(STEPS):
        rounded = adjoint.astype(jnp.bfloat16).reshape(1, blocks_dev, quarter, hidden)
        whole_rows = edge_exchange(rounded, quarters, False, 2, rounded)
        slot_sums = block_apply(
            backward_kernel, group_row, member, member_slot, weights_g, whole_rows,
            (slot_total, quarter, hidden),
        )
        arrived = lax.all_to_all(
            slot_sums, ("x", "c"), split_axis=0, concat_axis=0, tiled=True
        )
        dense = combine_apply(wanted_flat, arrived, blocks_dev)
        owned = lax.psum_scatter(dense, "z", scatter_dimension=0, tiled=True)
        adjoint = 0.9 * owned.reshape(row_count, hidden)
        factor = 0.1 if step_index + 1 < STEPS else 1.0
        gradient = gradient + factor * adjoint
    return (current, gradient)


def solution(mesh):
    devices = mesh.devices.reshape(Z_SIZE, X_SIZE, CORE_SIZE, mesh.shape["edge"])
    fine = Mesh(devices, ("z", "x", "c", "edge"))
    node = ("z", "x", "c")
    placed = (
        P((*node, "edge"), None),
        P((*node, "edge"), None),
        P(),
        P(node, None),
        P(node, None),
        P(node, None, "edge", None),
    )
    return jax.shard_map(
        per_device,
        mesh=fine,
        in_specs=placed,
        out_specs=(P((*node, "edge"), None), P((*node, "edge"), None)),
        check_vma=False,
    )
```

```python
import functools

import jax
import jax.numpy as jnp
from jax import lax
from jax.experimental import pallas as pl
from jax.experimental.pallas import tpu as pltpu
from jax.sharding import Mesh
from jax.sharding import PartitionSpec as P

MESH = pl.DeviceIdType.MESH

CAP = 2
STEPS = 2
Z_SIZE = 8
X_SIZE = 4
CORE_SIZE = 2
GROUP = 4
GROUPS_PER_STEP = 28
BLOCKS = 192


def forward_kernel(rows_ref, members_ref, slots_ref, v_ref, x_ref, out_ref):
    block_count = BLOCKS
    step = pl.program_id(0)
    quarters, _, quarter, hidden = out_ref.shape

    @pl.when(step == 0)
    def _():
        out_ref[...] = jnp.zeros_like(out_ref)

    def body(i, carry):
        g = step * GROUPS_PER_STEP + i

        j = rows_ref[g]
        pieces = []
        for m in range(GROUP):
            valid = members_ref[g * GROUP + m] < block_count
            piece = x_ref[slots_ref[g * GROUP + m]]
            pieces.append(jnp.where(valid, piece, jnp.zeros_like(piece)))
        sources = jnp.concatenate(pieces, axis=0)
        weights = v_ref[i]
        product = lax.dot_general(
            weights, sources, (((0,), (0,)), ((), ())), preferred_element_type=jnp.float32
        )
        out_ref[:, j] += product.reshape(quarters, quarter, hidden)
        return carry

    lax.fori_loop(0, GROUPS_PER_STEP, body, 0, unroll=7)


def backward_kernel(rows_ref, members_ref, slots_ref, v_ref, a_ref, out_ref):
    block_count = BLOCKS
    step = pl.program_id(0)
    quarters, _, quarter, hidden = a_ref.shape

    @pl.when(step == 0)
    def _():
        out_ref[...] = jnp.zeros_like(out_ref)

    def body(i, carry):
        g = step * GROUPS_PER_STEP + i

        j = rows_ref[g]
        sources = a_ref[:, j].reshape(quarters * quarter, hidden)
        weights = v_ref[i]
        product = jnp.dot(weights, sources, preferred_element_type=jnp.float32)
        for m in range(GROUP):
            s = slots_ref[g * GROUP + m]
            piece = product[m * quarter:(m + 1) * quarter]
            valid = members_ref[g * GROUP + m] < block_count
            out_ref[s] += jnp.where(valid, piece, jnp.zeros_like(piece))

        return carry

    lax.fori_loop(0, GROUPS_PER_STEP, body, 0, unroll=7)


def combine_kernel(want_ref, arrived_ref, out_ref):
    out_ref[...] = jnp.zeros_like(out_ref)
    lines = out_ref.shape[0]

    def body(q, carry):
        j = want_ref[q]
        piece = arrived_ref[q]
        out_ref[q // CAP % lines, jnp.maximum(j, 0)] += jnp.where(j >= 0, piece, jnp.zeros_like(piece))

        return carry

    lax.fori_loop(0, arrived_ref.shape[0], body, 0, unroll=16)


def edge_exchange_kernel(reduce, x_ref, out_ref, held, send_sem, recv_sem):
    count = held.shape[0]
    me = lax.axis_index("edge")
    barrier = pltpu.get_barrier_semaphore()
    for d in range(1, count):
        pl.semaphore_signal(
            barrier, inc=1, device_id={"edge": lax.rem(me + d, count)}, device_id_type=MESH
        )
    pl.semaphore_wait(barrier, count - 1)
    copies = []
    for d in range(1, count):
        peer = lax.rem(me + d, count)
        copy = pltpu.make_async_remote_copy(
            src_ref=x_ref.at[peer] if reduce else x_ref.at[0],
            dst_ref=held.at[me],
            send_sem=send_sem.at[d],
            recv_sem=recv_sem.at[d],
            device_id={"edge": peer},
            device_id_type=MESH,
        )
        copy.start()
        copies.append(copy)
    held[me] = x_ref[me] if reduce else x_ref[0]
    for copy in copies:
        copy.wait()
    if reduce:
        total = held[0]
        for q in range(1, count):
            total = total + held[q]
        out_ref[...] = total
    else:
        out_ref[...] = held[...]


def edge_exchange(chunks, count, reduce, collective_id):
    piece = chunks.shape[1:]
    out_shape = piece if reduce else (count,) + piece
    return pl.pallas_call(
        functools.partial(edge_exchange_kernel, reduce),
        out_shape=jax.ShapeDtypeStruct(out_shape, chunks.dtype),
        in_specs=[pl.BlockSpec(memory_space=pltpu.VMEM)],
        out_specs=pl.BlockSpec(memory_space=pltpu.VMEM),
        scratch_shapes=[
            pltpu.VMEM((count,) + piece, chunks.dtype),
            pltpu.SemaphoreType.DMA((count,)),
            pltpu.SemaphoreType.DMA((count,)),
        ],
        compiler_params=pltpu.CompilerParams(collective_id=collective_id, has_side_effects=True),
    )(chunks)


def block_apply(kernel, rows, members, slots, weights_g, dense, out_shape):
    group_count, depth, width = weights_g.shape
    return pl.pallas_call(
        kernel,
        out_shape=jax.ShapeDtypeStruct(out_shape, jnp.float32),
        grid_spec=pltpu.PrefetchScalarGridSpec(
            num_scalar_prefetch=3,
            grid=(group_count // GROUPS_PER_STEP,),
            in_specs=[
                pl.BlockSpec((GROUPS_PER_STEP, depth, width), lambda i, *_: (i, 0, 0)),
                pl.BlockSpec(dense.shape, lambda i, *_: (0,) * dense.ndim),
            ],
            out_specs=pl.BlockSpec(out_shape, lambda i, *_: (0,) * len(out_shape)),
        ),
        compiler_params=pltpu.CompilerParams(dimension_semantics=("arbitrary",)),
    )(rows, members, slots, weights_g, dense)


def combine_apply(wanted, arrived, blocks_dev):
    slot_total, quarter, hidden = arrived.shape
    lines = slot_total // (CAP * X_SIZE * CORE_SIZE)
    return pl.pallas_call(
        combine_kernel,
        out_shape=jax.ShapeDtypeStruct((lines, blocks_dev, quarter, hidden), jnp.float32),
        grid_spec=pltpu.PrefetchScalarGridSpec(
            num_scalar_prefetch=1,
            grid=(1,),
            in_specs=[pl.BlockSpec(arrived.shape, lambda i, w: (0, 0, 0))],
            out_specs=pl.BlockSpec(
                (lines, blocks_dev, quarter, hidden), lambda i, w: (0, 0, 0, 0)
            ),
        ),
    )(wanted, arrived)


def grouping(row_ids, blocks_dev):
    block_count = row_ids.shape[0]
    group_count = block_count // GROUP + blocks_dev
    hot = (row_ids[:, None] == jnp.arange(blocks_dev, dtype=jnp.int32)[None, :]).astype(jnp.float32)
    block_range = jnp.arange(block_count, dtype=jnp.int32)
    before = (block_range[None, :] < block_range[:, None]).astype(jnp.float32)
    rank = jnp.sum(
        jnp.dot(before, hot, precision=lax.Precision.HIGHEST) * hot, axis=1
    ).astype(jnp.int32)
    counts = jnp.sum(hot, axis=0).astype(jnp.int32)
    groups_per_row = (counts + GROUP - 1) // GROUP
    group_end = jnp.cumsum(groups_per_row)
    group_start = group_end - groups_per_row
    position = jnp.sum(hot * group_start[None, :].astype(jnp.float32), axis=1).astype(jnp.int32) * GROUP + rank
    member = jnp.full((group_count * GROUP,), block_count, jnp.int32).at[position].set(block_range)
    group_range = jnp.arange(group_count, dtype=jnp.int32)
    group_row = jnp.minimum(
        jnp.sum((group_range[:, None] >= group_end[None, :]).astype(jnp.int32), axis=1), blocks_dev - 1
    ).astype(jnp.int32)
    return member, group_row


def per_device(teleport, cotangent, fetch_table, block_row, block_slot, values):
    row_count, hidden = teleport.shape
    quarter = values.shape[2]
    blocks_dev = row_count // quarter
    slot_total = fetch_table.shape[1]
    quarters = lax.axis_size("edge")
    row_peers = X_SIZE * CORE_SIZE
    z_me = lax.axis_index("z")
    x_me = lax.axis_index("x")
    c_me = lax.axis_index("c")
    weights = values[0]
    row_ids = block_row[0]
    slot_ids = block_slot[0]

    owner = slot_ids // CAP
    placed_slots = (
        ((owner // CORE_SIZE % X_SIZE * CORE_SIZE + owner % CORE_SIZE) * Z_SIZE + owner // (CORE_SIZE * X_SIZE))
        * CAP
        + slot_ids % CAP
    ).astype(jnp.int32)

    peer_range = jnp.arange(row_peers, dtype=jnp.int32)
    z_range = jnp.arange(Z_SIZE, dtype=jnp.int32)
    peer_groups = (z_me * X_SIZE + peer_range // CORE_SIZE) * CORE_SIZE + peer_range % CORE_SIZE
    line_owners = (z_range * X_SIZE + x_me) * CORE_SIZE + c_me
    table_cols = line_owners[:, None] * CAP + jnp.arange(CAP, dtype=jnp.int32)[None, :]
    wanted = fetch_table[peer_groups[:, None, None], table_cols[None, :, :]]
    send_index = (z_range[None, :, None] * blocks_dev + jnp.maximum(wanted, 0)).reshape(-1)

    member, group_row = grouping(row_ids, blocks_dev)
    member_slot = jnp.take(placed_slots, member, axis=0, mode="clip")
    weights_g = jnp.take(weights, member, axis=0, mode="clip").reshape(
        member.shape[0] // GROUP, GROUP * quarter, weights.shape[2]
    )
    wanted_flat = wanted.reshape(-1)

    current = teleport
    for step_index in range(STEPS):
        rounded = current.astype(jnp.bfloat16).reshape(blocks_dev, quarter, hidden)
        line_blocks = lax.all_gather(rounded, "z", axis=0, tiled=True)
        outgoing = jnp.take(line_blocks, send_index, axis=0)
        received = lax.all_to_all(
            outgoing, ("x", "c"), split_axis=0, concat_axis=0, tiled=True
        )
        partial = block_apply(
            forward_kernel, group_row, member, member_slot, weights_g, received,
            (quarters, blocks_dev, quarter, hidden),
        )
        summed = edge_exchange(partial, quarters, True, 1)
        current = 0.9 * summed.reshape(row_count, hidden) + 0.1 * teleport

    adjoint = cotangent
    gradient = 0.1 * cotangent
    for step_index in range(STEPS):
        rounded = adjoint.astype(jnp.bfloat16).reshape(1, blocks_dev, quarter, hidden)
        whole_rows = edge_exchange(rounded, quarters, False, 2)
        slot_sums = block_apply(
            backward_kernel, group_row, member, member_slot, weights_g, whole_rows,
            (slot_total, quarter, hidden),
        )
        arrived = lax.all_to_all(
            slot_sums, ("x", "c"), split_axis=0, concat_axis=0, tiled=True
        )
        dense = combine_apply(wanted_flat, arrived, blocks_dev)
        owned = lax.psum_scatter(dense, "z", scatter_dimension=0, tiled=True)
        adjoint = 0.9 * owned.reshape(row_count, hidden)
        factor = 0.1 if step_index + 1 < STEPS else 1.0
        gradient = gradient + factor * adjoint
    return (current, gradient)


def solution(mesh):
    devices = mesh.devices.reshape(Z_SIZE, X_SIZE, CORE_SIZE, mesh.shape["edge"])
    fine = Mesh(devices, ("z", "x", "c", "edge"))
    node = ("z", "x", "c")
    placed = (
        P((*node, "edge"), None),
        P((*node, "edge"), None),
        P(),
        P(node, None),
        P(node, None),
        P(node, None, "edge", None),
    )
    return jax.shard_map(
        per_device,
        mesh=fine,
        in_specs=placed,
        out_specs=(P((*node, "edge"), None), P((*node, "edge"), None)),
        check_vma=False,
    )
```
